32 devices in a mesh: seq: 32 (over z, y, x, core), chan: 1.
Axes of the slice: x: 2, y: 2, z: 4, core: 2. Of those that a mesh axis runs over, the one named last changes fastest.
Arguments:
- proj_in: bfloat16 [5120, 3, 8192], P('seq', None, 'chan'), may hold values from -6 to 6
- short_taps: float32 [7, 3, 8192], P(None, None, 'chan'), may hold values from -2.4 to 2.4
- long_taps: float32 [128, 8192], P(None, 'chan'), may hold values from -0.5 to 0.5
- skip_gain: float32 [8192], P('chan'), may hold values from -1 to 1
- keep: int32 [8192], P('chan'), may hold values from 0 to 1, as said below
- w_out: bfloat16 [8192, 4096], P('chan', 'seq'), may hold values from -0.09375 to 0.09375
- grad_out: bfloat16 [5120, 4096], P('seq', 'chan'), may hold values from -6 to 6
Outputs:
- output: bfloat16 [5120, 4096], P('seq', 'chan')
- grad_proj_in: bfloat16 [5120, 3, 8192], P('seq', None, 'chan')
- grad_long_taps: float32 [128, 8192], P(None, 'chan')
- grad_short_taps: float32 [7, 3, 8192], P(None, None, 'chan')
- grad_skip_gain: float32 [8192], P('chan')
The draws below stay inside these ranges and needn't reach their ends.
Inputs may be any that keep to these rules, and one draw needn't show every extreme that they name: `keep`: in every aligned group of 16 consecutive channels exactly half of the entries are 1 and the rest 0.
All inputs are finite; a program needn't handle non-finite values.
Results may differ from the reference program's by a relative error of at most 0.012.
Values may be sent and summed in bfloat16 or wider, within the bound.
A program may use at most 192 MiB of HBM per device.

```python
import jax
import jax.numpy as jnp
from jax import lax

D = 8192
DOUT = 4096
TAPS = 128
SHORT = 7
GROUP = 16
TOKENS = 5120
CHAN_BLOCK = 8192
N_CHAN = 1


def draw_keep(key, part):
    order = jax.random.permutation(key, D).reshape(D // GROUP, GROUP)
    ranks = jnp.argsort(jnp.argsort(order, axis=1, stable=True), axis=1, stable=True)
    return (ranks < GROUP // 2).astype(jnp.int32).reshape(D)


def steps_of(key, extent, cuts, smallest, high):
    def one(position, shards_of):
        draws = jax.random.uniform(jax.random.fold_in(jax.random.fold_in(key, 6), position), (shards_of,), jnp.float32, smallest / len(cuts), high / len(cuts))
        return jnp.repeat(jnp.exp(draws), extent[position] // shards_of).reshape((-1,) + (1,) * (len(extent) - position - 1))

    gain = one(*cuts[0])
    for cut in cuts[1:]:
        gain = gain * one(*cut)
    return gain


def gaussian(own_key, extent, width, reach, pieces=(), kind=jnp.bfloat16):
    loudness = steps_of(own_key, extent, pieces, -0.22, 0.18) if pieces else 1.0
    drawn = jax.random.normal(own_key, extent, jnp.float32) * width * loudness
    return jnp.minimum(jnp.maximum(drawn, -reach), reach).astype(kind)


def setup_inputs(seed: int = 0) -> dict:
    streams_of = jax.random.split(jax.random.key(seed), 8)
    return {
        "proj_in": gaussian(streams_of[0], (TOKENS, 3, D), 1.0, 6.0, ((0, 32),)),
        "short_taps": gaussian(streams_of[1], (SHORT, 3, D), 0.4, 2.4, (), jnp.float32),
        "long_taps": gaussian(streams_of[2], (TAPS, D), TAPS ** -0.5, 0.5, (), jnp.float32),
        "skip_gain": jnp.clip(jax.random.uniform(streams_of[3], (D,), jnp.float32, -1.0, 1.0), -1.0, 1.0),
        "keep": draw_keep(jax.random.fold_in(streams_of[7], 71), 0),
        "w_out": gaussian(streams_of[5], (D, DOUT), (D // 2) ** -0.5, 0.09375, ((1, 32),)),
        "grad_out": gaussian(streams_of[6], (TOKENS, DOUT), 1.0, 6.0, ((0, 32),)),
    }


def shift_down(values, steps):
    if steps == 0:
        return values
    zero_rows = jnp.zeros((steps,) + values.shape[1:], values.dtype)
    return jnp.concatenate([zero_rows, values[:-steps]], axis=0)


def shift_up(values, steps):
    if steps == 0:
        return values
    zero_rows = jnp.zeros((steps,) + values.shape[1:], values.dtype)
    return jnp.concatenate([values[steps:], zero_rows], axis=0)


def causal_long(signal, filt):
    length = 2 * signal.shape[0]
    spectrum = jnp.fft.rfft(signal, n=length, axis=0) * jnp.fft.rfft(filt, n=length, axis=0)
    return jnp.fft.irfft(spectrum, n=length, axis=0)[: signal.shape[0]]


def lag_sums(later_part, earlier_part):
    length = 2 * later_part.shape[0]
    spectrum = jnp.fft.rfft(later_part, n=length, axis=0) * jnp.conj(jnp.fft.rfft(earlier_part, n=length, axis=0))
    return jnp.fft.irfft(spectrum, n=length, axis=0)[:TAPS]


def front_part(stream_block, short_block, long_block, gain_block):
    stream_f = stream_block.astype(jnp.float32)
    mixed = sum(short_block[j] * shift_down(stream_f, j) for j in range(SHORT))
    key_value = (mixed[:, 1] * mixed[:, 2]).astype(jnp.bfloat16)
    key_value_f = key_value.astype(jnp.float32)
    filtered = causal_long(key_value_f, long_block) + gain_block * key_value_f
    return stream_f, mixed, key_value_f, filtered


def forward_block(items):
    stream_block, short_block, long_block, gain_block, keep_block = items
    stream_f, mixed, key_value_f, filtered = front_part(stream_block, short_block, long_block, gain_block)
    return (mixed[:, 0] * filtered * keep_block).astype(jnp.bfloat16)


def backward_block(items):
    stream_block, short_block, long_block, gain_block, grad_block = items
    stream_f, mixed, key_value_f, filtered = front_part(stream_block, short_block, long_block, gain_block)
    grad_query = grad_block * filtered
    grad_filt = lax.optimization_barrier((grad_block * mixed[:, 0]).astype(jnp.bfloat16)).astype(jnp.float32)
    grad_key_value = causal_long(grad_filt[::-1], long_block)[::-1] + gain_block * grad_filt
    grad_long = lag_sums(grad_filt, key_value_f)
    grad_gain = jnp.sum(grad_filt * key_value_f, axis=0)
    grad_mixed = jnp.stack([grad_query, grad_key_value * mixed[:, 2], grad_key_value * mixed[:, 1]], axis=1)
    grad_mixed = lax.optimization_barrier(grad_mixed.astype(jnp.bfloat16)).astype(jnp.float32)
    grad_stream = sum(short_block[j] * shift_up(grad_mixed, j) for j in range(SHORT)).astype(jnp.bfloat16)
    grad_short = jnp.stack([jnp.sum(grad_mixed * shift_down(stream_f, j), axis=0) for j in range(SHORT)])
    return grad_stream, grad_long, grad_short, grad_gain


def reference(proj_in, short_taps, long_taps, skip_gain, keep, w_out, grad_out):
    block_width = min(512, D)
    block_count = D // block_width
    streams = proj_in.reshape(TOKENS, 3, block_count, block_width).transpose(2, 0, 1, 3)
    shorts = short_taps.reshape(SHORT, 3, block_count, block_width).transpose(2, 0, 1, 3)
    longs = long_taps.reshape(TAPS, block_count, block_width).transpose(1, 0, 2)
    gains = skip_gain.reshape(block_count, block_width)
    keep_f = keep.astype(jnp.float32)
    keeps = keep_f.reshape(block_count, block_width)
    gated = lax.map(forward_block, (streams, shorts, longs, gains, keeps))
    gated = gated.transpose(1, 0, 2).reshape(TOKENS, D)
    total = jnp.zeros((TOKENS, DOUT), jnp.float32)
    for index in range(N_CHAN):
        lower = index * CHAN_BLOCK
        term = jnp.dot(gated[:, lower:lower + CHAN_BLOCK], w_out[lower:lower + CHAN_BLOCK], preferred_element_type=jnp.float32)
        total = total + lax.optimization_barrier(term.astype(jnp.bfloat16)).astype(jnp.float32)
    output = total.astype(jnp.bfloat16)
    grad_gated = jnp.dot(grad_out, w_out.T, preferred_element_type=jnp.float32) * keep_f
    grads = grad_gated.reshape(TOKENS, block_count, block_width).transpose(1, 0, 2)
    grad_stream, grad_long, grad_short, grad_gain = lax.map(backward_block, (streams, shorts, longs, gains, grads))
    grad_proj_in = grad_stream.transpose(1, 2, 0, 3).reshape(TOKENS, 3, D)
    grad_long_taps = grad_long.transpose(1, 0, 2).reshape(TAPS, D)
    grad_short_taps = grad_short.transpose(1, 2, 0, 3).reshape(SHORT, 3, D)
    grad_skip_gain = grad_gain.reshape(D)
    return output, grad_proj_in, grad_long_taps, grad_short_taps, grad_skip_gain
```

```python
import functools

import jax
import jax.numpy as jnp
import numpy as np
from jax import lax
from jax.experimental import pallas as pl
from jax.experimental.pallas import tpu as pltpu
from jax.sharding import PartitionSpec as P

GROUP = 16
SUB = 8
EDGE = 16
BLOCK = 512
F32 = jnp.float32
BF16 = jnp.bfloat16


def shifted(x, axis, by):
    peers = lax.axis_size(axis)
    pairs = [(i, i + by) for i in range(peers) if 0 <= i + by < peers]
    return lax.ppermute(x, axis, pairs)


def tree_sum(parts, axis):
    peers = lax.axis_size(axis)
    if peers & (peers - 1) or parts.shape[0] % peers:
        return lax.psum(parts, axis)
    me = lax.axis_index(axis)
    bits = [1 << s for s in range(peers.bit_length() - 1)]
    for bit in bits:
        half = parts.shape[0] // 2
        upper = (me & bit) != 0
        low, high = parts[:half], parts[half:]
        pairs = [(i, i ^ bit) for i in range(peers)]
        got = lax.ppermute(jnp.where(upper, low, high), axis, pairs)
        parts = jnp.where(upper, high, low) + got
    for bit in reversed(bits):
        upper = (me & bit) != 0
        pairs = [(i, i ^ bit) for i in range(peers)]
        got = lax.ppermute(parts, axis, pairs)
        parts = jnp.concatenate([jnp.where(upper, got, parts), jnp.where(upper, parts, got)], axis=0)
    return parts


def tables(tokens, taps, short_len):
    per = tokens // SUB
    lag = short_len - 1
    size = tokens + taps
    order = (np.arange(SUB)[None, :] * per + np.arange(per)[:, None]).reshape(-1)
    freq = np.arange(size // 2) + 0.5
    angle = 2 * np.pi * freq[:, None] * np.arange(size)[None, :] / size
    matrix = np.concatenate([np.cos(angle), -np.sin(angle)], axis=0)
    spread = np.zeros(((per + lag) * SUB, EDGE + tokens))
    for v in range(-lag, per):
        for s in range(SUB):
            spread[(v + lag) * SUB + s, EDGE + s * per + v] = 1.0
    perm = np.zeros((tokens, tokens))
    perm[np.arange(tokens), order] = 1.0
    before = np.zeros((size, tokens))
    after = np.zeros((size, tokens))
    for row, token in enumerate(order):
        if token >= tokens - taps:
            before[:, row] = -matrix[:, token + taps]
        if token < taps:
            after[:, row] = matrix[:, tokens + token]
    return dict(
        spread=spread, perm=perm, own=matrix[:, order], own_taps=matrix[:, :taps], before=before, after=after,
        inv=matrix[:, order].T * (2.0 / size), inv_taps=matrix[:, :taps].T * (2.0 / size),
    )


def dot(a, b):
    return jnp.dot(a, b, preferred_element_type=F32)


def dot_nt(a, b):
    return lax.dot_general(a, b, (((1,), (1,)), ((), ())), preferred_element_type=F32)


def dot_tn(a, b):
    return lax.dot_general(a, b, (((0,), (0,)), ((), ())), preferred_element_type=F32)


def product(x, h, half):
    xr, xi, hr, hi = x[:half], x[half:], h[:half], h[half:]
    return jnp.concatenate([xr * hr - xi * hi, xr * hi + xi * hr], axis=0)


def product_conj(x, h, half):
    xr, xi, hr, hi = x[:half], x[half:], h[:half], h[half:]
    return jnp.concatenate([xr * hr + xi * hi, xi * hr - xr * hi], axis=0)


def selector(slot_row, wide):
    rows = lax.broadcasted_iota(jnp.int32, (wide // 2, wide), 0)
    return jnp.where(rows == slot_row, 1.0, 0.0).astype(BF16)


def split(x):
    high = x.astype(BF16)
    return high, (x - high.astype(F32)).astype(BF16)


def pack_kernel(slot_ref, w_ref, out_ref):
    block = min(BLOCK, w_ref.shape[0])
    for n in range(w_ref.shape[0] // block):
        at = slice(n * block, (n + 1) * block)
        out = slice(n * block // 2, (n + 1) * block // 2)
        out_ref[out, :] = dot(selector(slot_ref[:, at], block), w_ref[at, :]).astype(BF16)


def stage_partners(me, peers):
    def flip(value):
        return me + value * (1 - 2 * ((me // value) % 2))

    bits = [1 << s for s in range(peers.bit_length() - 1)]
    if len(bits) < 3:
        return [flip(value) for value in reversed(bits)]
    core = me % 2
    swap = [flip(bits[1]) * (1 - core) + flip(bits[2]) * core, flip(bits[2]) * (1 - core) + flip(bits[1]) * core]
    return [flip(value) for value in bits[3:]] + swap + [flip(bits[0])]


def piece_owner(me, peers, piece):
    stages = peers.bit_length() - 1
    at = me
    for k in reversed(range(stages)):
        if piece >> k & 1:
            at = stage_partners(at, peers)[k]
    return at


def mega_kernel(
    peers, kept_blocks, skew,
    slot_ref, x_ref, edge_ref, long_ref, short_ref, gain_ref,
    spread_ref, perm_ref, own_ref, taps_ref, before_ref, after_ref, inv_ref, invt_ref, go_ref, w_ref,
    out_ref, gp_ref, head_ref, gs_ref, sums_ref, small_out_ref,
    panel, go_s, acc, kvh, gfh, kvs, gfs,
    mixed_r, xp_r, filt_r, gated_r, kspec_r, hspec_r, gspec_r, gq_r, longp_r, small_r, pad,
    own_sem, ag_send, ag_recv, kv_send, kv_recv, gf_send, gf_recv,
):
    t = pl.program_id(0)
    last_step = pl.num_programs(0) - 1
    me = lax.axis_index("seq")
    partners = stage_partners(me, peers)
    stages = len(partners)
    units, _, unit_rows, features = panel.shape
    per_block = units // kept_blocks
    ring = mixed_r.shape[0]
    tokens, wide = kvs.shape[1:]
    per = tokens // SUB
    short_len = short_ref.shape[1]
    lag = short_len - 1
    taps = long_ref.shape[0]
    half = own_ref.shape[0] // 2
    aligned = features % 128 == 0

    def gather(u, k):
        return pltpu.make_async_remote_copy(
            src_ref=panel.at[u, pl.ds(0, 1 << k)], dst_ref=panel.at[u, pl.ds(1 << k, 1 << k)],
            send_sem=ag_send.at[u, k], recv_sem=ag_recv.at[u, k],
            device_id={"seq": partners[k]}, device_id_type=pl.DeviceIdType.MESH,
        )

    def kv_copy(b):
        return pltpu.make_async_remote_copy(
            src_ref=kvs.at[b], dst_ref=kvh.at[b], send_sem=kv_send.at[b], recv_sem=kv_recv.at[b],
            device_id={"seq": lax.rem(me + 1, peers)}, device_id_type=pl.DeviceIdType.MESH,
        )

    def gf_copy(b):
        return pltpu.make_async_remote_copy(
            src_ref=gfs.at[b], dst_ref=gfh.at[b], send_sem=gf_send.at[b], recv_sem=gf_recv.at[b],
            device_id={"seq": lax.rem(me + peers - 1, peers)}, device_id_type=pl.DeviceIdType.MESH,
        )

    has_left = me > 0
    has_right = me < peers - 1

    @pl.when(t == 0)
    def _():
        load = pltpu.make_async_copy(w_ref, panel.at[:, 0], own_sem)
        load.start()
        barrier = pltpu.get_barrier_semaphore()
        for partner in partners:
            pl.semaphore_signal(barrier, inc=1, device_id={"seq": partner}, device_id_type=pl.DeviceIdType.MESH)
        pl.semaphore_signal(
            barrier, inc=1, device_id={"seq": lax.rem(me + 1, peers)}, device_id_type=pl.DeviceIdType.MESH)
        pl.semaphore_signal(
            barrier, inc=1, device_id={"seq": lax.rem(me + peers - 1, peers)}, device_id_type=pl.DeviceIdType.MESH)
        pl.semaphore_wait(barrier, stages + 2)
        load.wait()

    def wave(w):
        for k in reversed(range(stages)):
            u = w - 2 * k

            @pl.when((u >= 0) & (u < units))
            def _():
                if k > 0:
                    gather(u, k - 1).wait_recv()
                gather(u, k).start()

    for i in range(per_block):
        if i == per_block // 2:
            break
        wave(t * per_block + i)

    mix_at = t - (skew - 3)
    fwd_at = t - (skew - 1)
    grad_at = t - skew
    back_at = t - (skew + 2)

    @pl.when((mix_at >= 1) & (mix_at <= kept_blocks) & has_right)
    def _():
        kv_copy(mix_at - 1).start()

    @pl.when((grad_at >= 1) & (grad_at <= kept_blocks) & has_left)
    def _():
        gf_copy(grad_at - 1).start()

    @pl.when(t == 0)
    def _():
        acc[...] = jnp.zeros_like(acc)
        if aligned:
            for r in range(peers):
                at = pl.multiple_of(piece_owner(me, peers, r) * features, features)
                go_s[:, r * features : (r + 1) * features] = dot(
                    perm_ref[...], go_ref[:, pl.ds(at, features)]).astype(BF16)
        else:
            go_s[...] = dot(perm_ref[...], go_ref[...]).astype(BF16)

    @pl.when((t == 0) & jnp.logical_not(has_left))
    def _():
        kvh[...] = jnp.zeros_like(kvh)

    @pl.when((t == 0) & jnp.logical_not(has_right))
    def _():
        gfh[...] = jnp.zeros_like(gfh)

    @pl.when((mix_at >= 0) & (mix_at < kept_blocks))
    def _():
        slot = lax.rem(mix_at, ring)
        pad[...] = jnp.zeros_like(pad)
        for i in range(3):
            pad[i * SUB : i * SUB + short_len, :] = short_ref[i]
        pad[3 * SUB : 3 * SUB + 1, :] = gain_ref[...]
        high, low = split(pad[...])
        rows = []
        for i in range(3):
            rows += [edge_ref[i], x_ref[i]]
        rows += [long_ref[...].astype(BF16), high, low]
        packed = dot_nt(jnp.concatenate(rows, axis=0), selector(slot_ref[...], x_ref.shape[2]))
        each = EDGE + tokens
        longp_r[slot] = packed[3 * each : 3 * each + taps].astype(BF16)
        base = 3 * each + taps
        small = packed[base : base + 4 * SUB] + packed[base + 4 * SUB : base + 8 * SUB]
        small_r[slot] = small
        small_out_ref[...] = small
        mixed = []
        for i in range(3):
            xp = packed[i * each : (i + 1) * each].astype(BF16)
            xp_r[slot, i] = xp
            ext = dot(spread_ref[...], xp)
            total = small[i * SUB : i * SUB + 1] * ext[lag * SUB : lag * SUB + tokens]
            for j in range(1, short_len):
                at = (lag - j) * SUB
                total += small[i * SUB + j : i * SUB + j + 1] * ext[at : at + tokens]
            mixed.append(total)
            mixed_r[slot, i] = total.astype(BF16)
        kvs[mix_at] = (mixed[1] * mixed[2]).astype(BF16)

    @pl.when((fwd_at >= 0) & (fwd_at < kept_blocks) & has_left)
    def _():
        kv_copy(fwd_at).wait_recv()

    @pl.when((fwd_at >= 0) & (fwd_at < kept_blocks))
    def _():
        slot = lax.rem(fwd_at, ring)
        kv = kvs[fwd_at]
        kspec = dot(own_ref[...], kv) + dot(before_ref[...], kvh[fwd_at])
        hspec = dot(taps_ref[...], longp_r[slot])
        spec = product(kspec, hspec, half)
        filtered = dot(inv_ref[...], spec.astype(BF16)) + small_r[slot, 3 * SUB : 3 * SUB + 1, :] * kv.astype(F32)
        filt_r[slot] = filtered.astype(BF16)
        gated_r[slot] = (mixed_r[slot, 0].astype(F32) * filtered).astype(BF16)
        kspec_r[slot] = kspec.astype(BF16)
        hspec_r[slot] = hspec.astype(BF16)

    for i in range(per_block // 2, per_block):
        wave(t * per_block + i)

    @pl.when((grad_at >= 0) & (grad_at < kept_blocks))
    def _():
        slot = lax.rem(grad_at, ring)
        first = grad_at * per_block
        for i in range(per_block):
            gather(first + i, stages - 1).wait_recv()
        gated = gated_r[slot]
        gi = None
        group = min(8, peers)
        for q in range(0, peers, group):
            tile = jnp.concatenate(
                [jnp.concatenate([panel[first + i, r] for r in range(q, q + group)], axis=1) for i in range(per_block)],
                axis=0)
            cols = slice(q * features, (q + group) * features)
            acc[:, cols] += dot(gated, tile)
            term = dot_nt(go_s[:, cols], tile)
            gi = term if gi is None else gi + term
        gq_r[slot] = (gi * filt_r[slot].astype(F32)).astype(BF16)
        gf = (gi * mixed_r[slot, 0].astype(F32)).astype(BF16)
        gfs[grad_at] = gf
        gspec = dot(own_ref[...], gf)
        gspec_r[slot] = gspec.astype(BF16)
        spec = product_conj(gspec, kspec_r[slot].astype(F32), half)
        sums_ref[:taps, :] = dot(invt_ref[...], spec.astype(BF16)).astype(BF16)
        gain = jnp.sum(gf.astype(F32) * kvs[grad_at].astype(F32), axis=0, keepdims=True)
        sums_ref[taps:, :] = jnp.broadcast_to(gain, (2 * SUB, gain.shape[1])).astype(BF16)

    @pl.when((back_at >= 0) & (back_at < kept_blocks) & has_right)
    def _():
        gf_copy(back_at).wait_recv()

    @pl.when((back_at >= 0) & (back_at < kept_blocks))
    def _():
        slot = lax.rem(back_at, ring)
        gspec = gspec_r[slot].astype(F32) + dot(after_ref[...], gfh[back_at])
        spec = product_conj(gspec, hspec_r[slot].astype(F32), half)
        small = small_r[slot]
        gkv = dot(inv_ref[...], spec.astype(BF16)) + small[3 * SUB : 3 * SUB + 1, :] * gfs[back_at].astype(F32)
        grads = (
            gq_r[slot],
            (gkv * mixed_r[slot, 2].astype(F32)).astype(BF16),
            (gkv * mixed_r[slot, 1].astype(F32)).astype(BF16),
        )
        last = lax.broadcasted_iota(jnp.int32, (SUB, wide), 0) == SUB - 1
        gs_ref[...] = jnp.zeros_like(gs_ref)
        for i in range(3):
            gmf = grads[i].astype(F32)
            ext = dot(spread_ref[...], xp_r[slot, i])
            rolled = []
            for u in range(lag):
                tile = gmf[u * SUB : (u + 1) * SUB]
                rolled.append(jnp.where(last, 0.0, pltpu.roll(tile, SUB - 1, axis=0)))
                head_ref[i, u : u + 1, :] = tile[0:1]
            head_ref[i, lag:, :] = jnp.zeros((SUB - lag, wide), F32)
            gme = jnp.concatenate([gmf] + rolled, axis=0)
            total = None
            for j in range(lag + 1):
                term = small[i * SUB + j : i * SUB + j + 1, :] * gme[j * SUB : j * SUB + tokens]
                total = term if total is None else total + term
                at = (lag - j) * SUB
                gs_ref[i * SUB + j : i * SUB + j + 1, :] = jnp.sum(gmf * ext[at : at + tokens], axis=0, keepdims=True)
            gp_ref[i] = dot_tn(perm_ref[...], total.astype(BF16)).astype(BF16)

    @pl.when(t == last_step)
    def _():
        if aligned:
            for r in range(peers):
                at = pl.multiple_of(piece_owner(me, peers, r) * features, features)
                part = acc[:, r * features : (r + 1) * features].astype(BF16)
                out_ref[:, pl.ds(at, features)] = dot_tn(perm_ref[...], part).astype(BF16)
        else:
            out_ref[...] = dot_tn(perm_ref[...], acc[...].astype(BF16)).astype(BF16)

        @pl.loop(0, units)
        def _(u):
            for k in range(stages):
                gather(u, k).wait_send()

    @pl.when((t == last_step) & has_right)
    def _():
        @pl.loop(0, kept_blocks)
        def _(b):
            kv_copy(b).wait_send()

    @pl.when((t == last_step) & has_left)
    def _():
        @pl.loop(0, kept_blocks)
        def _(b):
            gf_copy(b).wait_send()


def final_kernel(slot_ref, gp_ref, halo_ref, small_ref, sums_ref, gs_ref, out_ref, long_ref, short_ref, gain_ref, pad):
    tokens = gp_ref.shape[1]
    taps = long_ref.shape[0]
    short_len = short_ref.shape[1]
    wide = slot_ref.shape[1]
    pick = selector(slot_ref[...], wide)
    pad[0 : 2 * SUB, :] = jnp.zeros((2 * SUB, wide // 2), F32)
    rows = []
    for i in range(3):
        pad[2 * SUB :, :] = halo_ref[i]
        fix = None
        for j in range(1, short_len):
            term = small_ref[i * SUB + j : i * SUB + j + 1, :] * pad[j : j + 2 * SUB, :]
            fix = term if fix is None else fix + term
        keep = tokens - 2 * SUB
        rows += [gp_ref[i, :keep, :], (gp_ref[i, keep:, :].astype(F32) + fix).astype(BF16)]
    high, low = split(gs_ref[...])
    rows += [sums_ref[...], high, low]
    wide_rows = dot(jnp.concatenate(rows, axis=0), pick)
    for i in range(3):
        out_ref[i] = wide_rows[i * tokens : (i + 1) * tokens].astype(BF16)
    long_ref[...] = wide_rows[3 * tokens : 3 * tokens + taps]
    gain_ref[...] = wide_rows[3 * tokens + taps : 3 * tokens + taps + 1]
    base = 3 * tokens + taps + 2 * SUB
    for i in range(3):
        at = base + i * SUB
        short_ref[i] = wide_rows[at : at + short_len] + wide_rows[at + 4 * SUB : at + 4 * SUB + short_len]


def params(flops=0, moved=0):
    return dict(
        compiler_params=pltpu.CompilerParams(
            dimension_semantics=("arbitrary",), vmem_limit_bytes=56 * 2**20
        ),
        cost_estimate=pl.CostEstimate(flops=int(flops), bytes_accessed=int(moved), transcendentals=0),
    )


def local(proj_in, short_taps, long_taps, skip_gain, keep, w_out, grad_out):
    tokens, _, channels = proj_in.shape
    tap_count = long_taps.shape[0]
    short_len = short_taps.shape[0]
    lag = short_len - 1
    size = tokens + tap_count
    block = min(BLOCK, channels)
    wide = block // 2
    blocks = channels // block
    kept = channels // 2

    table = {name: jnp.asarray(value, BF16) for name, value in tables(tokens, tap_count, short_len).items()}

    x = proj_in.transpose(1, 0, 2)
    short = short_taps.transpose(1, 0, 2)
    groups = keep.reshape(channels // GROUP, GROUP)
    rank = jnp.cumsum(groups, axis=1) - 1
    base = (jnp.arange(channels // GROUP, dtype=jnp.int32) % (block // GROUP)) * (GROUP // 2)
    slot = jnp.where(groups == 1, rank + base[:, None], -1).reshape(1, channels)
    gain = skip_gain.reshape(1, channels)
    go = lax.all_gather(grad_out, "chan", axis=1, tiled=True)
    whole = pl.BlockSpec(memory_space=pltpu.VMEM)

    def two(rows, off=0, cols=wide):
        return pl.BlockSpec((rows, cols), lambda c: (0, c + off))

    def three(lead, rows, off=0, at=0, cols=wide):
        return pl.BlockSpec((lead, rows, cols), lambda c: (at, 0, c + off))

    def sds(shape, kind):
        return jax.ShapeDtypeStruct(shape, kind)

    features = w_out.shape[1]
    peers = lax.axis_size("seq")
    per_block = 2
    units = blocks * per_block
    unit_rows = wide // per_block
    group = 4 if blocks % 4 == 0 else 1
    packed = pl.pallas_call(
        pack_kernel,
        grid=(blocks // group,),
        in_specs=[two(1, 0, block * group), pl.BlockSpec((block * group, features), lambda c: (c, 0))],
        out_specs=pl.BlockSpec((wide * group, features), lambda c: (c, 0)),
        out_shape=sds((kept, features), BF16),
        name="pack",
        **params(channels * block * features, 3 * channels * features),
    )(slot, w_out).reshape(units, unit_rows, features)

    me = lax.axis_index("seq")
    owners = jnp.stack([jnp.asarray(piece_owner(me, peers, r), jnp.int32) for r in range(peers)])
    aligned = features % 128 == 0
    if not aligned:
        go = jnp.take(go.reshape(tokens, peers, features), owners, axis=1).reshape(tokens, peers * features)

    edge = shifted(x[:, tokens - EDGE :, :], "seq", 1)
    skew = 6
    ring = min(6, blocks)
    total_steps = blocks + skew + 3

    def step(off):
        return lambda t: jnp.minimum(jnp.maximum(t - off, 0), blocks - 1)

    def blk(shape, off):
        at = step(off)
        lead = (0,) * (len(shape) - 1)
        return pl.BlockSpec(shape, lambda t: lead + (at(t),))

    m_off, g_off, b_off = skew - 3, skew, skew + 2
    out, gp, head, gs, sums, small = pl.pallas_call(
        functools.partial(mega_kernel, peers, blocks, skew),
        grid=(total_steps,),
        in_specs=[
            blk((1, block), m_off), blk((3, tokens, block), m_off), blk((3, EDGE, block), m_off),
            blk((tap_count, block), m_off), blk((3, short_len, block), m_off), blk((1, block), m_off),
        ] + [whole] * 9 + [pl.BlockSpec(memory_space=pl.ANY)],
        out_specs=[
            whole, blk((3, tokens, wide), b_off), blk((3, SUB, wide), b_off), blk((3 * SUB, wide), b_off),
            blk((tap_count + 2 * SUB, wide), g_off), blk((4 * SUB, wide), m_off),
        ],
        out_shape=[
            sds((tokens, peers * features), BF16), sds((3, tokens, kept), BF16), sds((3, SUB, kept), F32),
            sds((3 * SUB, kept), F32), sds((tap_count + 2 * SUB, kept), BF16), sds((4 * SUB, kept), F32),
        ],
        scratch_shapes=[
            pltpu.VMEM((units, peers, unit_rows, features), BF16),
            pltpu.VMEM((tokens, peers * features), BF16),
            pltpu.VMEM((tokens, peers * features), F32),
            pltpu.VMEM((blocks, tokens, wide), BF16),
            pltpu.VMEM((blocks, tokens, wide), BF16),
            pltpu.VMEM((blocks, tokens, wide), BF16),
            pltpu.VMEM((blocks, tokens, wide), BF16),
            pltpu.VMEM((ring, 3, tokens, wide), BF16),
            pltpu.VMEM((ring, 3, EDGE + tokens, wide), BF16),
            pltpu.VMEM((ring, tokens, wide), BF16),
            pltpu.VMEM((ring, tokens, wide), BF16),
            pltpu.VMEM((ring, size, wide), BF16),
            pltpu.VMEM((ring, size, wide), BF16),
            pltpu.VMEM((ring, size, wide), BF16),
            pltpu.VMEM((ring, tokens, wide), BF16),
            pltpu.VMEM((ring, tap_count, wide), BF16),
            pltpu.VMEM((ring, 4 * SUB, wide), F32),
            pltpu.VMEM((4 * SUB, block), F32),
            pltpu.SemaphoreType.DMA,
            pltpu.SemaphoreType.DMA((units, peers.bit_length() - 1)),
            pltpu.SemaphoreType.DMA((units, peers.bit_length() - 1)),
            pltpu.SemaphoreType.DMA((blocks,)),
            pltpu.SemaphoreType.DMA((blocks,)),
            pltpu.SemaphoreType.DMA((blocks,)),
            pltpu.SemaphoreType.DMA((blocks,)),
        ],
        compiler_params=pltpu.CompilerParams(
            dimension_semantics=("arbitrary",), vmem_limit_bytes=63 * 2**20, collective_id=0, has_side_effects=True,
        ),
        cost_estimate=pl.CostEstimate(
            flops=4 * tokens * kept * peers * features, bytes_accessed=20 * tokens * channels, transcendentals=0),
        name="mega",
    )(
        slot, x, edge, long_taps, short, gain,
        *[table[k] for k in ("spread", "perm", "own", "own_taps", "before", "after", "inv", "inv_taps")], go, packed,
    )
    if not aligned:
        back = jnp.argsort(owners)
        out = jnp.take(out.reshape(tokens, peers, features), back, axis=1).reshape(tokens, peers * features)
    sums = lax.psum(sums, "seq")
    summed = lax.psum_scatter(out, "chan", scatter_dimension=1, tiled=True)
    output = summed.astype(F32).astype(BF16)
    halo = shifted(head, "seq", -1)
    lanes = 128
    gs = tree_sum(gs.reshape(3 * SUB, kept // lanes, lanes).transpose(1, 0, 2), "seq")
    gs = gs.transpose(1, 0, 2).reshape(3 * SUB, kept)
    gs = jnp.pad(gs, ((0, SUB), (0, 0)))
    grad_proj, grad_long, grad_short, grad_gain = pl.pallas_call(
        final_kernel,
        grid=(blocks,),
        in_specs=[two(1, 0, block), three(3, tokens), three(3, SUB), two(4 * SUB), two(tap_count + 2 * SUB), two(4 * SUB)],
        out_specs=[three(3, tokens, cols=block), two(tap_count, 0, block), three(3, short_len, cols=block), two(1, 0, block)],
        out_shape=[
            sds((3, tokens, channels), BF16), sds((tap_count, channels), F32), sds((3, short_len, channels), F32),
            sds((1, channels), F32),
        ],
        scratch_shapes=[pltpu.VMEM((3 * SUB, wide), F32)],
        name="final",
        **params(42 * 16 * channels, 300 * channels),
    )(slot, gp, halo, small, sums, gs)
    return (
        output,
        grad_proj.transpose(1, 0, 2),
        grad_long,
        grad_short.transpose(1, 0, 2),
        grad_gain.reshape(channels),
    )


def solution(mesh):
    placed = (
        P("seq", None, "chan"),
        P(None, None, "chan"),
        P(None, "chan"),
        P("chan"),
        P("chan"),
        P("chan", "seq"),
        P("seq", "chan"),
    )
    return jax.shard_map(
        local,
        mesh=mesh,
        in_specs=placed,
        out_specs=(
            P("seq", "chan"),
            P("seq", None, "chan"),
            P(None, "chan"),
            P(None, None, "chan"),
            P("chan"),
        ),
        check_vma=False,
    )
```

```python
import functools

import jax
import jax.numpy as jnp
import numpy as np
from jax import lax
from jax.experimental import pallas as pl
from jax.experimental.pallas import tpu as pltpu
from jax.sharding import PartitionSpec as P

GROUP = 16
SUB = 8
EDGE = 16
BLOCK = 512
PARTS = 4
EARLY = 0
LATE = 5
F32 = jnp.float32
BF16 = jnp.bfloat16


def shifted(x, axis, by):
    peers = lax.axis_size(axis)
    pairs = [(i, i + by) for i in range(peers) if 0 <= i + by < peers]
    return lax.ppermute(x, axis, pairs)


def tables(tokens, taps, short_len):
    per = tokens // SUB
    lag = short_len - 1
    size = tokens + taps
    order = (np.arange(SUB)[None, :] * per + np.arange(per)[:, None]).reshape(-1)
    freq = np.arange(size // 2) + 0.5
    angle = 2 * np.pi * freq[:, None] * np.arange(size)[None, :] / size
    matrix = np.concatenate([np.cos(angle), -np.sin(angle)], axis=0)
    spread = np.zeros(((per + lag) * SUB, EDGE + tokens))
    for v in range(-lag, per):
        for s in range(SUB):
            spread[(v + lag) * SUB + s, EDGE + s * per + v] = 1.0
    perm = np.zeros((tokens, tokens))
    perm[np.arange(tokens), order] = 1.0
    before = np.zeros((size, tokens))
    after = np.zeros((size, tokens))
    for row, token in enumerate(order):
        if token >= tokens - taps:
            before[:, row] = -matrix[:, token + taps]
        if token < taps:
            after[:, row] = matrix[:, tokens + token]
    return dict(
        spread=spread, perm=perm, own=matrix[:, order], own_taps=matrix[:, :taps], before=before, after=after,
        inv=matrix[:, order].T * (2.0 / size), inv_taps=matrix[:, :taps].T * (2.0 / size),
    )


def dot(a, b):
    return jnp.dot(a, b, preferred_element_type=F32)


def dot_nt(a, b):
    return lax.dot_general(a, b, (((1,), (1,)), ((), ())), preferred_element_type=F32)


def dot_tn(a, b):
    return lax.dot_general(a, b, (((0,), (0,)), ((), ())), preferred_element_type=F32)


def product(x, h, half):
    xr, xi, hr, hi = x[:half], x[half:], h[:half], h[half:]
    return jnp.concatenate([xr * hr - xi * hi, xr * hi + xi * hr], axis=0)


def product_conj(x, h, half):
    xr, xi, hr, hi = x[:half], x[half:], h[:half], h[half:]
    return jnp.concatenate([xr * hr + xi * hi, xi * hr - xr * hi], axis=0)


def selector(slot, kept):
    rows = lax.broadcasted_iota(jnp.int32, (kept, slot.shape[1]), 0)
    return jnp.where(rows == slot, 1.0, 0.0).astype(BF16)


def split(x):
    high = x.astype(BF16)
    return high, (x - high.astype(F32)).astype(BF16)


def pack_kernel(keep_ref, count_ref, w_ref, out_ref, slot_ref):
    block = count_ref.shape[0]
    many = w_ref.shape[0] // block
    kept = jnp.concatenate(
        [jnp.where(keep_ref[n] == 1, 1.0, 0.0) for n in range(many)] + [jnp.zeros((-many % SUB, block), F32)], axis=0)
    slots = jnp.where(kept == 1.0, dot(kept.astype(BF16), count_ref[...]) - 1.0, -1.0).astype(jnp.int32)
    for n in range(many):
        slot = slots[n : n + 1]
        slot_ref[n] = slot
        out_ref[n * block // 2 : (n + 1) * block // 2, :] = dot(
            selector(slot, block // 2), w_ref[n * block : (n + 1) * block, :]).astype(BF16)


def flipped(value, bits):
    at = value
    for bit in bits:
        at = at + bit * (1 - 2 * ((value // bit) % 2))
    return at


def piece_owner(me, peers, piece):
    depth = peers // 8
    place, rest = piece % depth, piece // depth
    mid, far, other = rest & 1, rest >> 1 & 1, rest >> 2
    core = me % 2
    if other:
        core = 1 - core
    at = flipped(me, [1]) if other else me
    one, two = flipped(at, [2]), flipped(at, [4])
    both = flipped(at, [2, 4])
    if mid and far:
        at = both
    elif mid:
        at = one * (1 - core) + two * core
    elif far:
        at = two * (1 - core) + one * core
    return at + 8 * (place - me // 8)


def piece_slot(me, peers, bits):
    slot = 0
    for i, bit in enumerate(bits):
        mine = (me // (1 << i)) % 2
        slot = slot + (bit + mine - 2 * bit * mine) * (peers // 2 if i == 0 else 1 << (i - 1))
    return slot


def mega_kernel(
    peers, kept_blocks, skew, team,
    slot_ref, x_ref, edge_ref, long_ref, short_ref, gain_ref,
    spread_ref, perm_ref, own_ref, taps_ref, before_ref, after_ref, inv_ref, invt_ref, go_ref, w_ref,
    out_ref, gp_ref, halo_ref, red_ref, small_out_ref,
    panel, go_s, acc, kvh, gfh, kvs, gfs,
    mixed_r, xp_r, filt_r, gated_r, kspec_r, hspec_r, gspec_r, gq_r, longp_r, small_r, pad,
    own_sem, ag_send, ag_recv, kv_send, kv_recv, gf_send, gf_recv,
    red, land, agb, red_send, red_recv, heads, head_send, head_recv, heads_in,
):
    t = pl.program_id(0)
    last_step = pl.num_programs(0) - 1
    me = lax.axis_index("seq")
    stages = peers.bit_length() - 1
    units, _, _, depth, unit_rows, features = panel.shape
    deep = depth.bit_length() - 1
    per_block = units // kept_blocks
    ring = mixed_r.shape[0]
    tokens, wide = kvs.shape[1:]
    per = tokens // SUB
    short_len = short_ref.shape[1]
    lag = short_len - 1
    taps = long_ref.shape[0]
    half = own_ref.shape[0] // 2
    aligned = features % 128 == 0

    core = me % 2
    mate = flipped(me, [1])
    near, side = flipped(me, [2]), flipped(me, [4])
    mid, far = near * (1 - core) + side * core, side * (1 - core) + near * core
    place = me // 8
    half_at = 2 * (place // 2)
    line = depth == 4
    inner = (place == 1) | (place == 2)
    outer = (place == 0) | (place == 3)
    if line:
        along = [
            (flipped(me, [8]), place, place, 1, None, None),
            (me + 8 * (3 - 2 * place), half_at, half_at, 2, inner, inner),
            (flipped(me, [8]), 2 - half_at, 2 - half_at, 2, inner, outer),
        ]
    else:
        along = [
            (flipped(me, [8 << i]), place // (1 << i) * (1 << i), place // (1 << i) * (1 << i), 1 << i, None, None)
            for i in range(deep)
        ]
    hops = len(along) + 3

    def stage_kind(k, late):
        if k >= hops - 2:
            return "far" if k == hops - 2 else "core"
        if late:
            return "mid" if k == 0 else k - 1
        return "mid" if k == hops - 3 else k

    def gather(u, k, late):
        kind = stage_kind(k, late)
        if kind == "core":
            src, dst, partner = panel.at[u, 0:2], panel.at[u, 2:4], mate
        elif kind == "far":
            src, dst, partner = panel.at[u, 0:1], panel.at[u, 1:2], far
        elif kind == "mid" and late:
            src, dst, partner = panel.at[u, 0, 0, pl.ds(place, 1)], panel.at[u, 0, 1, pl.ds(place, 1)], mid
        elif kind == "mid":
            src, dst, partner = panel.at[u, 0, 0:1], panel.at[u, 0, 1:2], mid
        else:
            partner, low, to, count = along[kind][:4]
            lead = pl.ds(0, 2 if late else 1)
            src, dst = panel.at[u, 0, lead, pl.ds(low, count)], panel.at[u, 0, lead, pl.ds(to, count)]
        return pltpu.make_async_remote_copy(
            src_ref=src, dst_ref=dst, send_sem=ag_send.at[u, k], recv_sem=ag_recv.at[u, k],
            device_id={"seq": partner}, device_id_type=pl.DeviceIdType.MESH,
        )

    def when(cond, todo):
        if cond is None:
            todo()
        else:
            pl.when(cond)(todo)

    def sends(k, late):
        kind = stage_kind(k, late)
        return along[kind][4] if isinstance(kind, int) else None

    def receives(k, late):
        kind = stage_kind(k, late)
        return along[kind][5] if isinstance(kind, int) else None

    def both(u, todo):
        for late in (False, True):
            @pl.when((lax.rem(u, LATE if line else 2) > 0) == late)
            def _():
                todo(late)

    def kv_copy(b):
        return pltpu.make_async_remote_copy(
            src_ref=kvs.at[b], dst_ref=kvh.at[b], send_sem=kv_send.at[b], recv_sem=kv_recv.at[b],
            device_id={"seq": lax.rem(me + 1, peers)}, device_id_type=pl.DeviceIdType.MESH,
        )

    def gf_copy(b):
        return pltpu.make_async_remote_copy(
            src_ref=gfs.at[b], dst_ref=gfh.at[b], send_sem=gf_send.at[b], recv_sem=gf_recv.at[b],
            device_id={"seq": lax.rem(me + peers - 1, peers)}, device_id_type=pl.DeviceIdType.MESH,
        )

    part_rows = red_ref.shape[0] // PARTS

    def put_parts(b, low, values):
        for n in range(values.shape[0] // part_rows):
            rows = slice(n * part_rows, (n + 1) * part_rows)
            out_rows = slice((low + n) * part_rows, (low + n + 1) * part_rows)
            if not team:
                red_ref[out_rows, pl.ds(pl.multiple_of(b * wide, wide), wide)] = values[rows]
                continue
            member = lax.rem(b, team)
            for h in range(2):
                bits = [(low + n) % 2, (low + n) // 2, h] + [
                    (member // (1 << i)) % 2 for i in range(team.bit_length() - 1)]
                red[lax.div(b, team), piece_slot(me, peers, bits)] = values[rows, h * (wide // 2) : (h + 1) * (wide // 2)]

    chips = peers // 2
    others = [flipped(me, [2 << n for n in range(stages - 1) if q >> n & 1]) for q in range(chips)]

    def piece_copy(g, phase, src, dst, device):
        return pltpu.make_async_remote_copy(
            src_ref=src, dst_ref=dst, send_sem=red_send.at[g, phase], recv_sem=red_recv.at[g, phase],
            device_id={"seq": device}, device_id_type=pl.DeviceIdType.MESH,
        )

    def halves(g):
        return piece_copy(g, 0, red.at[g, pl.ds(chips, chips)], land.at[g, pl.ds(0, chips)], mate)

    def sums_to(g, q):
        return piece_copy(g, 1, red.at[g, pl.ds(q, 1)], land.at[g, pl.ds(chips + q, 1)], others[q])

    def all_sums(g):
        return piece_copy(g, 1, red.at[g, pl.ds(1, chips - 1)], land.at[g, pl.ds(chips + 1, chips - 1)], others[1])

    def total_to(g, q):
        return piece_copy(g, 2, agb.at[g, pl.ds(0, 1)], agb.at[g, pl.ds(q, 1)], others[q])

    def all_totals(g):
        return piece_copy(g, 2, red.at[g, pl.ds(1, chips - 1)], agb.at[g, pl.ds(1, chips - 1)], others[1])

    def whole_totals(g):
        return piece_copy(g, 3, agb.at[g, pl.ds(0, chips)], agb.at[g, pl.ds(chips, chips)], mate)

    def reduce_step():
        if not team:
            return
        final = kept_blocks // team - 1
        for s, pause in enumerate((0, 2, 4, 6, 7)):
            since = t - (team + skew + 1) - pause
            at_end = t == kept_blocks + skew + 1 + s
            g = jnp.where(at_end, final, lax.div(since, team))

            @pl.when(at_end | ((since >= 0) & (lax.rem(since, team) == 0) & (g < final)))
            def _():
                if s == 0:
                    halves(g).start()
                elif s == 1:
                    halves(g).wait_recv()
                    total = red[g, pl.ds(0, chips)].astype(F32) + land[g, pl.ds(0, chips)].astype(F32)
                    red[g, pl.ds(0, chips)] = total.astype(BF16)
                    for q in range(1, chips):
                        sums_to(g, q).start()
                elif s == 2:
                    all_sums(g).wait_recv()
                    total = red[g, 0].astype(F32)
                    for q in range(1, chips):
                        total += land[g, chips + q].astype(F32)
                    agb[g, 0] = total.astype(BF16)
                    for q in range(1, chips):
                        total_to(g, q).start()
                elif s == 3:
                    all_totals(g).wait_recv()
                    whole_totals(g).start()
                else:
                    whole_totals(g).wait_recv()
                    for p in range(peers):
                        bits = [p >> n & 1 for n in range(stages)]
                        rows = slice((p % PARTS) * part_rows, (p % PARTS + 1) * part_rows)
                        lanes = wide // 2
                        at = pl.multiple_of((g * (2 * team) + p // PARTS) * lanes, lanes)
                        red_ref[rows, pl.ds(at, lanes)] = agb[g, piece_slot(me, peers, bits)]

    def head_copy(b):
        return pltpu.make_async_remote_copy(
            src_ref=heads.at[b], dst_ref=heads_in.at[b], send_sem=head_send.at[b], recv_sem=head_recv.at[b],
            device_id={"seq": lax.rem(me + peers - 1, peers)}, device_id_type=pl.DeviceIdType.MESH,
        )

    has_left = me > 0
    has_right = me < peers - 1

    @pl.when(t == 0)
    def _():
        load = pltpu.make_async_copy(w_ref, panel.at[:, 0, 0, place], own_sem)
        load.start()
        barrier = pltpu.get_barrier_semaphore()
        for partner in others[1:] + [mate]:
            pl.semaphore_signal(barrier, inc=1, device_id={"seq": partner}, device_id_type=pl.DeviceIdType.MESH)
        pl.semaphore_signal(
            barrier, inc=1, device_id={"seq": lax.rem(me + 1, peers)}, device_id_type=pl.DeviceIdType.MESH)
        pl.semaphore_signal(
            barrier, inc=1, device_id={"seq": lax.rem(me + peers - 1, peers)}, device_id_type=pl.DeviceIdType.MESH)
        pl.semaphore_wait(barrier, chips + 2)
        load.wait()

    ahead = [3 + 2 * (len(along) - k) - (k == 0) for k in range(len(along))] + [3, 0, -2]

    def wave(w):
        for k in reversed(range(hops)):
            upto = jnp.minimum(w + ahead[k] + 1, units)
            start = jnp.where(w == k, 0, w + ahead[k])

            @pl.when((w >= k) & (start < upto))
            def _():
                @pl.loop(start, upto)
                def _(u):
                    def todo(late):
                        if k > 0:
                            when(receives(k - 1, late), lambda: gather(u, k - 1, late).wait_recv())
                        when(sends(k, late), lambda: gather(u, k, late).start())

                    both(u, todo)

    @pl.when(t == 0)
    def _():
        pl.loop(0, EARLY)(wave)

    for i in range(per_block // 2):
        wave(EARLY + t * per_block + i)
    reduce_step()

    mix_at = t - (skew - 3)
    fwd_at = t - (skew - 1)
    grad_at = t - (skew - 1)
    back_at = t - (skew + 1)

    @pl.when((mix_at >= 1) & (mix_at <= kept_blocks) & has_right)
    def _():
        kv_copy(mix_at - 1).start()

    @pl.when((grad_at >= 1) & (grad_at <= kept_blocks) & has_left)
    def _():
        gf_copy(grad_at - 1).start()

    @pl.when((back_at >= 1) & (back_at <= kept_blocks) & has_left)
    def _():
        head_copy(back_at - 1).start()

    @pl.when(t == 0)
    def _():
        acc[...] = jnp.zeros_like(acc)
        if aligned:
            for r in range(peers):
                at = pl.multiple_of(piece_owner(me, peers, r) * features, features)
                go_s[:, r * features : (r + 1) * features] = dot(
                    perm_ref[...], go_ref[:, pl.ds(at, features)]).astype(BF16)
        else:
            go_s[...] = dot(perm_ref[...], go_ref[...]).astype(BF16)

    @pl.when((t == 0) & jnp.logical_not(has_left))
    def _():
        kvh[...] = jnp.zeros_like(kvh)

    @pl.when((t == 0) & jnp.logical_not(has_right))
    def _():
        gfh[...] = jnp.zeros_like(gfh)
        heads_in[...] = jnp.zeros_like(heads_in)

    @pl.when((mix_at >= 0) & (mix_at < kept_blocks))
    def _():
        slot = lax.rem(mix_at, ring)
        pad[...] = jnp.zeros_like(pad)
        for i in range(3):
            pad[i * SUB : i * SUB + short_len, :] = short_ref[i]
        pad[3 * SUB : 3 * SUB + 1, :] = gain_ref[...]
        high, low = split(pad[...])
        rows = []
        for i in range(3):
            rows += [edge_ref[i], x_ref[i]]
        rows += [long_ref[...].astype(BF16), high, low]
        packed = dot_nt(jnp.concatenate(rows, axis=0), selector(slot_ref[0], wide))
        each = EDGE + tokens
        longp_r[slot] = packed[3 * each : 3 * each + taps].astype(BF16)
        base = 3 * each + taps
        small = packed[base : base + 4 * SUB] + packed[base + 4 * SUB : base + 8 * SUB]
        small_r[slot] = small
        small_out_ref[...] = small
        mixed = []
        for i in range(3):
            xp = packed[i * each : (i + 1) * each].astype(BF16)
            xp_r[slot, i] = xp
            ext = dot(spread_ref[...], xp)
            total = small[i * SUB : i * SUB + 1] * ext[lag * SUB : lag * SUB + tokens]
            for j in range(1, short_len):
                at = (lag - j) * SUB
                total += small[i * SUB + j : i * SUB + j + 1] * ext[at : at + tokens]
            mixed.append(total)
            mixed_r[slot, i] = total.astype(BF16)
        kvs[mix_at] = (mixed[1] * mixed[2]).astype(BF16)

    @pl.when((fwd_at >= 0) & (fwd_at < kept_blocks) & has_left)
    def _():
        kv_copy(fwd_at).wait_recv()

    @pl.when((fwd_at >= 0) & (fwd_at < kept_blocks))
    def _():
        slot = lax.rem(fwd_at, ring)
        kv = kvs[fwd_at]
        kspec = dot(own_ref[...], kv) + dot(before_ref[...], kvh[fwd_at])
        hspec = dot(taps_ref[...], longp_r[slot])
        spec = product(kspec, hspec, half)
        filtered = dot(inv_ref[...], spec.astype(BF16)) + small_r[slot, 3 * SUB : 3 * SUB + 1, :] * kv.astype(F32)
        filt_r[slot] = filtered.astype(BF16)
        gated_r[slot] = (mixed_r[slot, 0].astype(F32) * filtered).astype(BF16)
        kspec_r[slot] = kspec.astype(BF16)
        hspec_r[slot] = hspec.astype(BF16)

    for i in range(per_block // 2, per_block):
        wave(EARLY + t * per_block + i)

    @pl.when((grad_at >= 0) & (grad_at < kept_blocks))
    def _():
        slot = lax.rem(grad_at, ring)
        first = grad_at * per_block
        for i in range(per_block):
            gather(first + i, hops - 1, False).wait_recv()
        gated = gated_r[slot]
        gi = None
        group = min(8, peers)
        for q in range(0, peers, group):
            tile = jnp.concatenate(
                [
                    jnp.concatenate([
                        panel[first + i, r // (2 * depth), r // depth % 2, r % depth] for r in range(q, q + group)
                    ], axis=1)
                    for i in range(per_block)
                ],
                axis=0)
            cols = slice(q * features, (q + group) * features)
            acc[:, cols] += dot(gated, tile)
            term = dot_nt(go_s[:, cols], tile)
            gi = term if gi is None else gi + term
        gq_r[slot] = (gi * filt_r[slot].astype(F32)).astype(BF16)
        gf = (gi * mixed_r[slot, 0].astype(F32)).astype(BF16)
        gfs[grad_at] = gf
        gspec = dot(own_ref[...], gf)
        gspec_r[slot] = gspec.astype(BF16)
        spec = product_conj(gspec, kspec_r[slot].astype(F32), half)
        gain = jnp.sum(gf.astype(F32) * kvs[grad_at].astype(F32), axis=0, keepdims=True)
        gain = jnp.broadcast_to(gain, ((PARTS - 1) * part_rows - taps, wide))
        sums = jnp.concatenate([dot(invt_ref[...], spec.astype(BF16)), gain], axis=0)
        put_parts(grad_at, 0, sums.astype(BF16))

    @pl.when((back_at >= 0) & (back_at < kept_blocks) & has_right)
    def _():
        gf_copy(back_at).wait_recv()

    @pl.when((back_at >= 0) & (back_at < kept_blocks))
    def _():
        slot = lax.rem(back_at, ring)
        gspec = gspec_r[slot].astype(F32) + dot(after_ref[...], gfh[back_at])
        spec = product_conj(gspec, hspec_r[slot].astype(F32), half)
        small = small_r[slot]
        gkv = dot(inv_ref[...], spec.astype(BF16)) + small[3 * SUB : 3 * SUB + 1, :] * gfs[back_at].astype(F32)
        grads = (
            gq_r[slot],
            (gkv * mixed_r[slot, 2].astype(F32)).astype(BF16),
            (gkv * mixed_r[slot, 1].astype(F32)).astype(BF16),
        )
        last = lax.broadcasted_iota(jnp.int32, (SUB, wide), 0) == SUB - 1
        gs = []
        for i in range(3):
            gmf = grads[i].astype(F32)
            ext = dot(spread_ref[...], xp_r[slot, i])
            rolled = []
            for u in range(lag):
                tile = gmf[u * SUB : (u + 1) * SUB]
                rolled.append(jnp.where(last, 0.0, pltpu.roll(tile, SUB - 1, axis=0)))
                heads[back_at, i, u : u + 1, :] = tile[0:1]
            heads[back_at, i, lag:, :] = jnp.zeros((SUB - lag, wide), F32)
            gme = jnp.concatenate([gmf] + rolled, axis=0)
            total = None
            for j in range(lag + 1):
                term = small[i * SUB + j : i * SUB + j + 1, :] * gme[j * SUB : j * SUB + tokens]
                total = term if total is None else total + term
                at = (lag - j) * SUB
                gs.append(jnp.sum(gmf * ext[at : at + tokens], axis=0, keepdims=True))
            gs += [jnp.zeros((1, wide), F32)] * (SUB - short_len)
            gp_ref[i] = dot_tn(perm_ref[...], total.astype(BF16)).astype(BF16)
        gs.append(jnp.zeros((part_rows - 3 * SUB, wide), F32))
        put_parts(back_at, PARTS - 1, jnp.concatenate(gs, axis=0).astype(BF16))

    share = peers // 4
    for n in range(4):
        @pl.when(grad_at == kept_blocks + 2 + n)
        def _():
            for r in range(n * share, (n + 1) * share):
                part = acc[:, r * features : (r + 1) * features].astype(BF16)
                part = dot_tn(perm_ref[...], part).astype(BF16)
                if aligned:
                    out_ref[:, pl.ds(pl.multiple_of(piece_owner(me, peers, r) * features, features), features)] = part
                else:
                    out_ref[:, r * features : (r + 1) * features] = part

    @pl.when(t == last_step)
    def _():
        @pl.loop(0, units)
        def _(u):
            for k in range(hops):
                both(u, lambda late: when(sends(k, late), lambda: gather(u, k, late).wait_send()))

        if team:
            @pl.loop(0, kept_blocks // team)
            def _(g):
                halves(g).wait_send()
                all_sums(g).wait_send()
                all_totals(g).wait_send()
                whole_totals(g).wait_send()

    @pl.when((t == last_step) & has_right)
    def _():
        @pl.loop(0, kept_blocks)
        def _(b):
            kv_copy(b).wait_send()
            head_copy(b).wait_recv()

    @pl.when((t == last_step) & has_left)
    def _():
        @pl.loop(0, kept_blocks)
        def _(b):
            gf_copy(b).wait_send()
            head_copy(b).wait_send()

    @pl.when(t == last_step)
    def _():
        halo_ref[...] = heads_in[...]


def final_kernel(slot_ref, gp_ref, halo_ref, small_ref, red_ref, out_ref, long_ref, short_ref, gain_ref, pad):
    tokens = gp_ref.shape[1]
    taps = long_ref.shape[0]
    short_len = short_ref.shape[1]
    block = slot_ref.shape[2]
    keep = tokens - 2 * SUB
    for n in range(slot_ref.shape[0]):
        to = slice(n * block, (n + 1) * block)
        at = slice(n * block // 2, (n + 1) * block // 2)
        pick = selector(slot_ref[n], block // 2)
        pad[n, 0 : 2 * SUB, :] = jnp.zeros((2 * SUB, block // 2), F32)
        rows = []
        for i in range(3):
            pad[n, 2 * SUB :, :] = halo_ref[n, i]
            fix = None
            for j in range(1, short_len):
                term = small_ref[i * SUB + j : i * SUB + j + 1, at] * pad[n, j : j + 2 * SUB, :]
                fix = term if fix is None else fix + term
            rows += [gp_ref[i, :keep, at], (gp_ref[i, keep:, at].astype(F32) + fix).astype(BF16)]
        rows += [red_ref[:, at]]
        wide_rows = dot(jnp.concatenate(rows, axis=0), pick)
        for i in range(3):
            out_ref[i, :, to] = wide_rows[i * tokens : (i + 1) * tokens].astype(BF16)
        long_ref[:, to] = wide_rows[3 * tokens : 3 * tokens + taps]
        gain_ref[:, to] = wide_rows[3 * tokens + taps : 3 * tokens + taps + 1]
        base = 3 * tokens + red_ref.shape[0] // PARTS * (PARTS - 1)
        for i in range(3):
            short_ref[i, :, to] = wide_rows[base + i * SUB : base + i * SUB + short_len]


def params(flops=0, moved=0):
    return dict(
        compiler_params=pltpu.CompilerParams(
            dimension_semantics=("arbitrary",), vmem_limit_bytes=56 * 2**20
        ),
        cost_estimate=pl.CostEstimate(flops=int(flops), bytes_accessed=int(moved), transcendentals=0),
    )


def local(proj_in, short_taps, long_taps, skip_gain, keep, w_out, grad_out):
    tokens, _, channels = proj_in.shape
    tap_count = long_taps.shape[0]
    short_len = short_taps.shape[0]
    lag = short_len - 1
    size = tokens + tap_count
    block = min(BLOCK, channels)
    wide = block // 2
    blocks = channels // block
    kept = channels // 2

    table = {name: jnp.asarray(value, BF16) for name, value in tables(tokens, tap_count, short_len).items()}

    x = proj_in.transpose(1, 0, 2)
    short = short_taps.transpose(1, 0, 2)
    keep = keep.reshape(blocks, 1, block)
    count = jnp.asarray(np.triu(np.ones((block, block))), BF16)
    gain = skip_gain.reshape(1, channels)
    go = lax.all_gather(grad_out, "chan", axis=1, tiled=True)
    whole = pl.BlockSpec(memory_space=pltpu.VMEM)

    def two(rows, off=0, cols=wide):
        return pl.BlockSpec((rows, cols), lambda c: (0, c + off))

    def three(lead, rows, off=0, at=0, cols=wide):
        return pl.BlockSpec((lead, rows, cols), lambda c: (at, 0, c + off))

    def sds(shape, kind):
        return jax.ShapeDtypeStruct(shape, kind)

    features = w_out.shape[1]
    peers = lax.axis_size("seq")
    per_block = 2
    units = blocks * per_block
    unit_rows = wide // per_block
    group = 4 if blocks % 4 == 0 else 1
    packed, slot = pl.pallas_call(
        pack_kernel,
        grid=(blocks // group,),
        in_specs=[
            pl.BlockSpec((group, 1, block), lambda c: (c, 0, 0)), whole,
            pl.BlockSpec((block * group, features), lambda c: (c, 0)),
        ],
        out_specs=[
            pl.BlockSpec((wide * group, features), lambda c: (c, 0)), pl.BlockSpec((group, 1, block), lambda c: (c, 0, 0)),
        ],
        out_shape=[sds((kept, features), BF16), sds((blocks, 1, block), jnp.int32)],
        name="pack",
        **params(channels * block * features, 3 * channels * features),
    )(keep, count, w_out)
    packed = packed.reshape(units, unit_rows, features)

    me = lax.axis_index("seq")
    owners = jnp.stack([jnp.asarray(piece_owner(me, peers, r), jnp.int32) for r in range(peers)])
    aligned = features % 128 == 0
    if not aligned:
        go = jnp.take(go.reshape(tokens, peers, features), owners, axis=1).reshape(tokens, peers * features)

    edge = shifted(x[:, tokens - EDGE :, :], "seq", 1)
    skew = 3
    ring = min(6, blocks)
    part_rows = (tap_count + SUB + 2 * SUB * (PARTS - 1)) // (2 * SUB * (PARTS - 1)) * 2 * SUB
    team = peers // (2 * PARTS)
    if wide % 256 or team == 0 or blocks % team or peers & (peers - 1) or team * 2 * PARTS != peers:
        team = 0
    teams = blocks // team if team else 1
    slots = peers if team else 1
    hops = 6 if peers == 32 else peers.bit_length() - 1
    total_steps = blocks + skew + 6

    def step(off):
        return lambda t: jnp.minimum(jnp.maximum(t - off, 0), blocks - 1)

    def blk(shape, off):
        at = step(off)
        lead = (0,) * (len(shape) - 1)
        return pl.BlockSpec(shape, lambda t: lead + (at(t),))

    m_off, b_off = skew - 3, skew + 1
    out, gp, halo, red, small = pl.pallas_call(
        functools.partial(mega_kernel, peers, blocks, skew, team),
        grid=(total_steps,),
        in_specs=[
            pl.BlockSpec((1, 1, block), lambda t: (step(m_off)(t), 0, 0)), blk((3, tokens, block), m_off), blk((3, EDGE, block), m_off),
            blk((tap_count, block), m_off), blk((3, short_len, block), m_off), blk((1, block), m_off),
        ] + [whole] * 9 + [pl.BlockSpec(memory_space=pl.ANY)],
        out_specs=[
            whole, blk((3, tokens, wide), b_off), whole, whole, blk((4 * SUB, wide), m_off),
        ],
        out_shape=[
            sds((tokens, peers * features), BF16), sds((3, tokens, kept), BF16), sds((blocks, 3, SUB, wide), F32),
            sds((PARTS * part_rows, kept), BF16), sds((4 * SUB, kept), F32),
        ],
        scratch_shapes=[
            pltpu.VMEM((units, 4, 2, peers // 8, unit_rows, features), BF16),
            pltpu.VMEM((tokens, peers * features), BF16),
            pltpu.VMEM((tokens, peers * features), F32),
            pltpu.VMEM((blocks, tokens, wide), BF16),
            pltpu.VMEM((blocks, tokens, wide), BF16),
            pltpu.VMEM((blocks, tokens, wide), BF16),
            pltpu.VMEM((blocks, tokens, wide), BF16),
            pltpu.VMEM((ring, 3, tokens, wide), BF16),
            pltpu.VMEM((ring, 3, EDGE + tokens, wide), BF16),
            pltpu.VMEM((ring, tokens, wide), BF16),
            pltpu.VMEM((ring, tokens, wide), BF16),
            pltpu.VMEM((ring, size, wide), BF16),
            pltpu.VMEM((ring, size, wide), BF16),
            pltpu.VMEM((ring, size, wide), BF16),
            pltpu.VMEM((ring, tokens, wide), BF16),
            pltpu.VMEM((ring, tap_count, wide), BF16),
            pltpu.VMEM((ring, 4 * SUB, wide), F32),
            pltpu.VMEM((4 * SUB, block), F32),
            pltpu.SemaphoreType.DMA,
            pltpu.SemaphoreType.DMA((units, hops)),
            pltpu.SemaphoreType.DMA((units, hops)),
            pltpu.SemaphoreType.DMA((blocks,)),
            pltpu.SemaphoreType.DMA((blocks,)),
            pltpu.SemaphoreType.DMA((blocks,)),
            pltpu.SemaphoreType.DMA((blocks,)),
            pltpu.VMEM((teams, slots, part_rows, wide // 2), BF16),
            pltpu.VMEM((teams, slots, part_rows, wide // 2), BF16),
            pltpu.VMEM((teams, slots, part_rows, wide // 2), BF16),
            pltpu.SemaphoreType.DMA((teams, 4)),
            pltpu.SemaphoreType.DMA((teams, 4)),
            pltpu.VMEM((blocks, 3, SUB, wide), F32),
            pltpu.SemaphoreType.DMA((blocks,)),
            pltpu.SemaphoreType.DMA((blocks,)),
            pltpu.VMEM((blocks, 3, SUB, wide), F32),
        ],
        compiler_params=pltpu.CompilerParams(
            dimension_semantics=("arbitrary",), vmem_limit_bytes=63 * 2**20, collective_id=0, has_side_effects=True,
        ),
        cost_estimate=pl.CostEstimate(
            flops=4 * tokens * kept * peers * features, bytes_accessed=20 * tokens * channels, transcendentals=0),
        name="mega",
    )(
        slot, x, edge, long_taps, short, gain,
        *[table[k] for k in ("spread", "perm", "own", "own_taps", "before", "after", "inv", "inv_taps")], go, packed,
    )
    if not aligned:
        back = jnp.argsort(owners)
        out = jnp.take(out.reshape(tokens, peers, features), back, axis=1).reshape(tokens, peers * features)
    if not team:
        red = lax.psum(red, "seq")
    summed = lax.psum_scatter(out, "chan", scatter_dimension=1, tiled=True)
    output = summed.astype(F32).astype(BF16)
    pair = 2 if blocks % 2 == 0 else 1
    many, few = pair * block, pair * wide
    grad_proj, grad_long, grad_short, grad_gain = pl.pallas_call(
        final_kernel,
        grid=(blocks // pair,),
        in_specs=[
            pl.BlockSpec((pair, 1, block), lambda c: (c, 0, 0)), three(3, tokens, cols=few),
            pl.BlockSpec((pair, 3, SUB, wide), lambda c: (c, 0, 0, 0)), two(4 * SUB, 0, few), two(PARTS * part_rows, 0, few),
        ],
        out_specs=[three(3, tokens, cols=many), two(tap_count, 0, many), three(3, short_len, cols=many), two(1, 0, many)],
        out_shape=[
            sds((3, tokens, channels), BF16), sds((tap_count, channels), F32), sds((3, short_len, channels), F32),
            sds((1, channels), F32),
        ],
        scratch_shapes=[pltpu.VMEM((pair, 3 * SUB, wide), F32)],
        name="final",
        **params(42 * 16 * channels, 300 * channels),
    )(slot, gp, halo, small, red)
    return (
        output,
        grad_proj.transpose(1, 0, 2),
        grad_long,
        grad_short.transpose(1, 0, 2),
        grad_gain.reshape(channels),
    )


def solution(mesh):
    placed = (
        P("seq", None, "chan"),
        P(None, None, "chan"),
        P(None, "chan"),
        P("chan"),
        P("chan"),
        P("chan", "seq"),
        P("seq", "chan"),
    )
    return jax.shard_map(
        local,
        mesh=mesh,
        in_specs=placed,
        out_specs=(
            P("seq", "chan"),
            P("seq", None, "chan"),
            P(None, "chan"),
            P(None, None, "chan"),
            P("chan"),
        ),
        check_vma=False,
    )
```

```python
import functools

import jax
import jax.numpy as jnp
import numpy as np
from jax import lax
from jax.experimental import pallas as pl
from jax.experimental.pallas import tpu as pltpu
from jax.sharding import PartitionSpec as P

GROUP = 16
SUB = 8
EDGE = 16
BLOCK = 512
PARTS = 4
EARLY = 0
LATE = 5
F32 = jnp.float32
BF16 = jnp.bfloat16


def shifted(x, axis, by):
    peers = lax.axis_size(axis)
    pairs = [(i, i + by) for i in range(peers) if 0 <= i + by < peers]
    return lax.ppermute(x, axis, pairs)


def tables(tokens, taps, short_len):
    per = tokens // SUB
    lag = short_len - 1
    size = tokens + taps
    order = (np.arange(SUB)[None, :] * per + np.arange(per)[:, None]).reshape(-1)
    freq = np.arange(size // 2) + 0.5
    angle = 2 * np.pi * freq[:, None] * np.arange(size)[None, :] / size
    matrix = np.concatenate([np.cos(angle), -np.sin(angle)], axis=0)
    spread = np.zeros(((per + lag) * SUB, EDGE + tokens))
    for v in range(-lag, per):
        for s in range(SUB):
            spread[(v + lag) * SUB + s, EDGE + s * per + v] = 1.0
    perm = np.zeros((tokens, tokens))
    perm[np.arange(tokens), order] = 1.0
    before = np.zeros((size, tokens))
    after = np.zeros((size, tokens))
    for row, token in enumerate(order):
        if token >= tokens - taps:
            before[:, row] = -matrix[:, token + taps]
        if token < taps:
            after[:, row] = matrix[:, tokens + token]
    return dict(
        spread=spread, perm=perm, own=matrix[:, order], own_taps=matrix[:, :taps], before=before, after=after,
        inv=matrix[:, order].T * (2.0 / size), inv_taps=matrix[:, :taps].T * (2.0 / size),
    )


def dot(a, b):
    return jnp.dot(a, b, preferred_element_type=F32)


def dot_nt(a, b):
    return lax.dot_general(a, b, (((1,), (1,)), ((), ())), preferred_element_type=F32)


def dot_tn(a, b):
    return lax.dot_general(a, b, (((0,), (0,)), ((), ())), preferred_element_type=F32)


def product(x, h, half):
    xr, xi, hr, hi = x[:half], x[half:], h[:half], h[half:]
    return jnp.concatenate([xr * hr - xi * hi, xr * hi + xi * hr], axis=0)


def product_conj(x, h, half):
    xr, xi, hr, hi = x[:half], x[half:], h[:half], h[half:]
    return jnp.concatenate([xr * hr + xi * hi, xi * hr - xr * hi], axis=0)


def selector(slot, kept):
    rows = lax.broadcasted_iota(jnp.int32, (kept, slot.shape[1]), 0)
    return jnp.where(rows == slot, 1.0, 0.0).astype(BF16)


def split(x):
    high = x.astype(BF16)
    return high, (x - high.astype(F32)).astype(BF16)


def pack_kernel(keep_ref, count_ref, w_ref, out_ref, slot_ref):
    block = count_ref.shape[0]
    many = w_ref.shape[0] // block
    kept = jnp.concatenate(
        [jnp.where(keep_ref[n] == 1, 1.0, 0.0) for n in range(many)] + [jnp.zeros((-many % SUB, block), F32)], axis=0)
    slots = jnp.where(kept == 1.0, dot(kept.astype(BF16), count_ref[...]) - 1.0, -1.0).astype(jnp.int32)
    for n in range(many):
        slot = slots[n : n + 1]
        slot_ref[n] = slot
        out_ref[n * block // 2 : (n + 1) * block // 2, :] = dot(
            selector(slot, block // 2), w_ref[n * block : (n + 1) * block, :]).astype(BF16)


def flipped(value, bits):
    at = value
    for bit in bits:
        at = at + bit * (1 - 2 * ((value // bit) % 2))
    return at


def piece_owner(me, peers, piece):
    depth = peers // 8
    place, rest = piece % depth, piece // depth
    mid, far, other = rest & 1, rest >> 1 & 1, rest >> 2
    core = me % 2
    if other:
        core = 1 - core
    at = flipped(me, [1]) if other else me
    one, two = flipped(at, [2]), flipped(at, [4])
    both = flipped(at, [2, 4])
    if mid and far:
        at = both
    elif mid:
        at = one * (1 - core) + two * core
    elif far:
        at = two * (1 - core) + one * core
    return at + 8 * (place - me // 8)


def piece_slot(me, peers, bits):
    slot = 0
    for i, bit in enumerate(bits):
        mine = (me // (1 << i)) % 2
        weight = (peers // 2, peers // 8, peers // 4)[i] if i < 3 else 1 << (i - 3)
        slot = slot + (bit + mine - 2 * bit * mine) * weight
    return slot


def mega_kernel(
    peers, kept_blocks, skew, team,
    slot_ref, x_ref, edge_ref, long_ref, short_ref, gain_ref,
    spread_ref, perm_ref, own_ref, taps_ref, before_ref, after_ref, inv_ref, invt_ref, go_ref, w_ref,
    out_ref, gp_ref, halo_ref, red_ref, small_out_ref,
    panel, go_s, acc, kvh, gfh, kvs, gfs,
    mixed_r, xp_r, filt_r, gated_r, kspec_r, hspec_r, gspec_r, gq_r, longp_r, small_r, pad,
    own_sem, ag_send, ag_recv, kv_send, kv_recv, gf_send, gf_recv,
    red, land, agb, red_send, red_recv, heads, head_send, head_recv, heads_in,
):
    t = pl.program_id(0)
    last_step = pl.num_programs(0) - 1
    me = lax.axis_index("seq")
    stages = peers.bit_length() - 1
    units, _, _, depth, unit_rows, features = panel.shape
    deep = depth.bit_length() - 1
    per_block = units // kept_blocks
    ring = mixed_r.shape[0]
    tokens, wide = kvs.shape[1:]
    per = tokens // SUB
    short_len = short_ref.shape[1]
    lag = short_len - 1
    taps = long_ref.shape[0]
    half = own_ref.shape[0] // 2
    aligned = features % 128 == 0

    core = me % 2
    mate = flipped(me, [1])
    near, side = flipped(me, [2]), flipped(me, [4])
    mid, far = near * (1 - core) + side * core, side * (1 - core) + near * core
    place = me // 8
    half_at = 2 * (place // 2)
    line = depth == 4
    inner = (place == 1) | (place == 2)
    outer = (place == 0) | (place == 3)
    if line:
        along = [
            (flipped(me, [8]), place, place, 1, None, None),
            (me + 8 * (3 - 2 * place), half_at, half_at, 2, inner, inner),
            (flipped(me, [8]), 2 - half_at, 2 - half_at, 2, inner, outer),
        ]
    else:
        along = [
            (flipped(me, [8 << i]), place // (1 << i) * (1 << i), place // (1 << i) * (1 << i), 1 << i, None, None)
            for i in range(deep)
        ]
    hops = len(along) + 3

    def stage_kind(k, late):
        if k >= hops - 2:
            return "far" if k == hops - 2 else "core"
        if late:
            return "mid" if k == 0 else k - 1
        return "mid" if k == hops - 3 else k

    def gather(u, k, late):
        kind = stage_kind(k, late)
        if kind == "core":
            src, dst, partner = panel.at[u, 0:2], panel.at[u, 2:4], mate
        elif kind == "far":
            src, dst, partner = panel.at[u, 0:1], panel.at[u, 1:2], far
        elif kind == "mid" and late:
            src, dst, partner = panel.at[u, 0, 0, pl.ds(place, 1)], panel.at[u, 0, 1, pl.ds(place, 1)], mid
        elif kind == "mid":
            src, dst, partner = panel.at[u, 0, 0:1], panel.at[u, 0, 1:2], mid
        else:
            partner, low, to, count = along[kind][:4]
            lead = pl.ds(0, 2 if late else 1)
            src, dst = panel.at[u, 0, lead, pl.ds(low, count)], panel.at[u, 0, lead, pl.ds(to, count)]
        return pltpu.make_async_remote_copy(
            src_ref=src, dst_ref=dst, send_sem=ag_send.at[u, k], recv_sem=ag_recv.at[u, k],
            device_id={"seq": partner}, device_id_type=pl.DeviceIdType.MESH,
        )

    def when(cond, todo):
        if cond is None:
            todo()
        else:
            pl.when(cond)(todo)

    def sends(k, late):
        kind = stage_kind(k, late)
        return along[kind][4] if isinstance(kind, int) else None

    def receives(k, late):
        kind = stage_kind(k, late)
        return along[kind][5] if isinstance(kind, int) else None

    def both(u, todo):
        for late in (False, True):
            @pl.when((lax.rem(u, LATE if line else 2) > 0) == late)
            def _():
                todo(late)

    def kv_copy(b):
        return pltpu.make_async_remote_copy(
            src_ref=kvs.at[b], dst_ref=kvh.at[b], send_sem=kv_send.at[b], recv_sem=kv_recv.at[b],
            device_id={"seq": lax.rem(me + 1, peers)}, device_id_type=pl.DeviceIdType.MESH,
        )

    def gf_copy(b):
        return pltpu.make_async_remote_copy(
            src_ref=gfs.at[b], dst_ref=gfh.at[b], send_sem=gf_send.at[b], recv_sem=gf_recv.at[b],
            device_id={"seq": lax.rem(me + peers - 1, peers)}, device_id_type=pl.DeviceIdType.MESH,
        )

    part_rows = red_ref.shape[0] // PARTS

    def put_parts(b, low, values):
        for n in range(values.shape[0] // part_rows):
            rows = slice(n * part_rows, (n + 1) * part_rows)
            out_rows = slice((low + n) * part_rows, (low + n + 1) * part_rows)
            if not team:
                red_ref[out_rows, pl.ds(pl.multiple_of(b * wide, wide), wide)] = values[rows]
                continue
            member = lax.rem(b, team)
            for h in range(2):
                bits = [(low + n) % 2, (low + n) // 2, h] + [
                    (member // (1 << i)) % 2 for i in range(team.bit_length() - 1)]
                red[lax.div(b, team), piece_slot(me, peers, bits)] = values[rows, h * (wide // 2) : (h + 1) * (wide // 2)]

    chips = peers // 2
    others = [flipped(me, [2 << n for n in range(stages - 1) if q >> n & 1]) for q in range(chips)]

    def piece_copy(g, phase, src, dst, device):
        return pltpu.make_async_remote_copy(
            src_ref=src, dst_ref=dst, send_sem=red_send.at[g, phase], recv_sem=red_recv.at[g, phase],
            device_id={"seq": device}, device_id_type=pl.DeviceIdType.MESH,
        )

    def halves(g):
        return piece_copy(g, 0, red.at[g, pl.ds(chips, chips)], land.at[g, pl.ds(0, chips)], mate)

    def plane_to(g, m):
        rows = pl.ds(m * depth, depth)
        return piece_copy(g, 1, red.at[g, rows], land.at[g, pl.ds(chips + m * depth, depth)], others[m])

    def plane_all(g):
        rows = pl.ds(depth, 3 * depth)
        return piece_copy(g, 1, red.at[g, rows], land.at[g, pl.ds(chips + depth, 3 * depth)], others[1])

    def column_to(g, q):
        return piece_copy(g, 2, red.at[g, pl.ds(q, 1)], land.at[g, pl.ds(chips + q, 1)], others[4 * q])

    def column_all(g):
        return piece_copy(g, 2, red.at[g, pl.ds(1, depth - 1)], land.at[g, pl.ds(chips + 1, depth - 1)], others[4])

    def total_to(g, q):
        return piece_copy(g, 3, agb.at[g, pl.ds(0, 1)], agb.at[g, pl.ds(q, 1)], others[4 * q])

    def total_all(g):
        return piece_copy(g, 3, red.at[g, pl.ds(1, depth - 1)], agb.at[g, pl.ds(1, depth - 1)], others[4])

    def totals_to(g, m):
        return piece_copy(g, 4, agb.at[g, pl.ds(0, depth)], agb.at[g, pl.ds(m * depth, depth)], others[m])

    def totals_all(g):
        return piece_copy(g, 4, red.at[g, pl.ds(depth, 3 * depth)], agb.at[g, pl.ds(depth, 3 * depth)], others[1])

    def whole_totals(g):
        return piece_copy(g, 5, agb.at[g, pl.ds(0, chips)], agb.at[g, pl.ds(chips, chips)], mate)

    def reduce_step():
        if not team:
            return
        final = kept_blocks // team - 1
        for s, pause in enumerate((0, 2, 4, 6, 7, 8, 9)):
            since = t - (team + skew + 1) - pause
            at_end = t == kept_blocks + skew + 1 + s
            g = jnp.where(at_end, final, lax.div(since, team))

            @pl.when(at_end | ((since >= 0) & (lax.rem(since, team) == 0) & (g < final)))
            def _():
                if s == 0:
                    halves(g).start()
                elif s == 1:
                    halves(g).wait_recv()
                    total = red[g, pl.ds(0, chips)].astype(F32) + land[g, pl.ds(0, chips)].astype(F32)
                    red[g, pl.ds(0, chips)] = total.astype(BF16)
                    for m in range(1, 4):
                        plane_to(g, m).start()
                elif s == 2:
                    plane_all(g).wait_recv()
                    total = red[g, pl.ds(0, depth)].astype(F32)
                    for m in range(1, 4):
                        total += land[g, pl.ds(chips + m * depth, depth)].astype(F32)
                    red[g, pl.ds(0, depth)] = total.astype(BF16)
                    for q in range(1, depth):
                        column_to(g, q).start()
                elif s == 3:
                    column_all(g).wait_recv()
                    total = red[g, 0].astype(F32)
                    for q in range(1, depth):
                        total += land[g, chips + q].astype(F32)
                    agb[g, 0] = total.astype(BF16)
                    for q in range(1, depth):
                        total_to(g, q).start()
                elif s == 4:
                    total_all(g).wait_recv()
                    for m in range(1, 4):
                        totals_to(g, m).start()
                elif s == 5:
                    totals_all(g).wait_recv()
                    whole_totals(g).start()
                else:
                    whole_totals(g).wait_recv()
                    for p in range(peers):
                        bits = [p >> n & 1 for n in range(stages)]
                        rows = slice((p % PARTS) * part_rows, (p % PARTS + 1) * part_rows)
                        lanes = wide // 2
                        at = pl.multiple_of((g * (2 * team) + p // PARTS) * lanes, lanes)
                        red_ref[rows, pl.ds(at, lanes)] = agb[g, piece_slot(me, peers, bits)]

    def head_copy(b):
        return pltpu.make_async_remote_copy(
            src_ref=heads.at[b], dst_ref=heads_in.at[b], send_sem=head_send.at[b], recv_sem=head_recv.at[b],
            device_id={"seq": lax.rem(me + peers - 1, peers)}, device_id_type=pl.DeviceIdType.MESH,
        )

    has_left = me > 0
    has_right = me < peers - 1

    @pl.when(t == 0)
    def _():
        load = pltpu.make_async_copy(w_ref, panel.at[:, 0, 0, place], own_sem)
        load.start()
        barrier = pltpu.get_barrier_semaphore()
        for partner in others[1:] + [mate]:
            pl.semaphore_signal(barrier, inc=1, device_id={"seq": partner}, device_id_type=pl.DeviceIdType.MESH)
        pl.semaphore_signal(
            barrier, inc=1, device_id={"seq": lax.rem(me + 1, peers)}, device_id_type=pl.DeviceIdType.MESH)
        pl.semaphore_signal(
            barrier, inc=1, device_id={"seq": lax.rem(me + peers - 1, peers)}, device_id_type=pl.DeviceIdType.MESH)
        pl.semaphore_wait(barrier, chips + 2)
        load.wait()

    ahead = [3 + 2 * (len(along) - k) - (k == 0) for k in range(len(along))] + [3, 0, -2]

    def wave(w):
        for k in reversed(range(hops)):
            upto = jnp.minimum(w + ahead[k] + 1, units)
            start = jnp.where(w == k, 0, w + ahead[k])

            @pl.when((w >= k) & (start < upto))
            def _():
                @pl.loop(start, upto)
                def _(u):
                    def todo(late):
                        if k > 0:
                            when(receives(k - 1, late), lambda: gather(u, k - 1, late).wait_recv())
                        when(sends(k, late), lambda: gather(u, k, late).start())

                    both(u, todo)

    @pl.when(t == 0)
    def _():
        pl.loop(0, EARLY)(wave)

    for i in range(per_block // 2):
        wave(EARLY + t * per_block + i)
    reduce_step()

    mix_at = t - (skew - 3)
    fwd_at = t - (skew - 1)
    grad_at = t - (skew - 1)
    back_at = t - (skew + 1)

    @pl.when((mix_at >= 1) & (mix_at <= kept_blocks) & has_right)
    def _():
        kv_copy(mix_at - 1).start()

    @pl.when((grad_at >= 1) & (grad_at <= kept_blocks) & has_left)
    def _():
        gf_copy(grad_at - 1).start()

    @pl.when((back_at >= 1) & (back_at <= kept_blocks) & has_left)
    def _():
        head_copy(back_at - 1).start()

    @pl.when(t == 0)
    def _():
        acc[...] = jnp.zeros_like(acc)
        if aligned:
            for r in range(peers):
                at = pl.multiple_of(piece_owner(me, peers, r) * features, features)
                go_s[:, r * features : (r + 1) * features] = dot(
                    perm_ref[...], go_ref[:, pl.ds(at, features)]).astype(BF16)
        else:
            go_s[...] = dot(perm_ref[...], go_ref[...]).astype(BF16)

    @pl.when((t == 0) & jnp.logical_not(has_left))
    def _():
        kvh[...] = jnp.zeros_like(kvh)

    @pl.when((t == 0) & jnp.logical_not(has_right))
    def _():
        gfh[...] = jnp.zeros_like(gfh)
        heads_in[...] = jnp.zeros_like(heads_in)

    @pl.when((mix_at >= 0) & (mix_at < kept_blocks))
    def _():
        slot = lax.rem(mix_at, ring)
        pad[...] = jnp.zeros_like(pad)
        for i in range(3):
            pad[i * SUB : i * SUB + short_len, :] = short_ref[i]
        pad[3 * SUB : 3 * SUB + 1, :] = gain_ref[...]
        high, low = split(pad[...])
        rows = []
        for i in range(3):
            rows += [edge_ref[i], x_ref[i]]
        rows += [long_ref[...].astype(BF16), high, low]
        packed = dot_nt(jnp.concatenate(rows, axis=0), selector(slot_ref[0], wide))
        each = EDGE + tokens
        longp_r[slot] = packed[3 * each : 3 * each + taps].astype(BF16)
        base = 3 * each + taps
        small = packed[base : base + 4 * SUB] + packed[base + 4 * SUB : base + 8 * SUB]
        small_r[slot] = small
        small_out_ref[...] = small
        mixed = []
        for i in range(3):
            xp = packed[i * each : (i + 1) * each].astype(BF16)
            xp_r[slot, i] = xp
            ext = dot(spread_ref[...], xp)
            total = small[i * SUB : i * SUB + 1] * ext[lag * SUB : lag * SUB + tokens]
            for j in range(1, short_len):
                at = (lag - j) * SUB
                total += small[i * SUB + j : i * SUB + j + 1] * ext[at : at + tokens]
            mixed.append(total)
            mixed_r[slot, i] = total.astype(BF16)
        kvs[mix_at] = (mixed[1] * mixed[2]).astype(BF16)

    @pl.when((fwd_at >= 0) & (fwd_at < kept_blocks) & has_left)
    def _():
        kv_copy(fwd_at).wait_recv()

    @pl.when((fwd_at >= 0) & (fwd_at < kept_blocks))
    def _():
        slot = lax.rem(fwd_at, ring)
        kv = kvs[fwd_at]
        kspec = dot(own_ref[...], kv) + dot(before_ref[...], kvh[fwd_at])
        hspec = dot(taps_ref[...], longp_r[slot])
        spec = product(kspec, hspec, half)
        filtered = dot(inv_ref[...], spec.astype(BF16)) + small_r[slot, 3 * SUB : 3 * SUB + 1, :] * kv.astype(F32)
        filt_r[slot] = filtered.astype(BF16)
        gated_r[slot] = (mixed_r[slot, 0].astype(F32) * filtered).astype(BF16)
        kspec_r[slot] = kspec.astype(BF16)
        hspec_r[slot] = hspec.astype(BF16)

    for i in range(per_block // 2, per_block):
        wave(EARLY + t * per_block + i)

    @pl.when((grad_at >= 0) & (grad_at < kept_blocks))
    def _():
        slot = lax.rem(grad_at, ring)
        first = grad_at * per_block
        for i in range(per_block):
            gather(first + i, hops - 1, False).wait_recv()
        gated = gated_r[slot]
        gi = None
        group = min(8, peers)
        for q in range(0, peers, group):
            tile = jnp.concatenate(
                [
                    jnp.concatenate([
                        panel[first + i, r // (2 * depth), r // depth % 2, r % depth] for r in range(q, q + group)
                    ], axis=1)
                    for i in range(per_block)
                ],
                axis=0)
            cols = slice(q * features, (q + group) * features)
            acc[:, cols] += dot(gated, tile)
            term = dot_nt(go_s[:, cols], tile)
            gi = term if gi is None else gi + term
        gq_r[slot] = (gi * filt_r[slot].astype(F32)).astype(BF16)
        gf = (gi * mixed_r[slot, 0].astype(F32)).astype(BF16)
        gfs[grad_at] = gf
        gspec = dot(own_ref[...], gf)
        gspec_r[slot] = gspec.astype(BF16)
        spec = product_conj(gspec, kspec_r[slot].astype(F32), half)
        gain = jnp.sum(gf.astype(F32) * kvs[grad_at].astype(F32), axis=0, keepdims=True)
        gain = jnp.broadcast_to(gain, ((PARTS - 1) * part_rows - taps, wide))
        sums = jnp.concatenate([dot(invt_ref[...], spec.astype(BF16)), gain], axis=0)
        put_parts(grad_at, 0, sums.astype(BF16))

    @pl.when((back_at >= 0) & (back_at < kept_blocks) & has_right)
    def _():
        gf_copy(back_at).wait_recv()

    @pl.when((back_at >= 0) & (back_at < kept_blocks))
    def _():
        slot = lax.rem(back_at, ring)
        gspec = gspec_r[slot].astype(F32) + dot(after_ref[...], gfh[back_at])
        spec = product_conj(gspec, hspec_r[slot].astype(F32), half)
        small = small_r[slot]
        gkv = dot(inv_ref[...], spec.astype(BF16)) + small[3 * SUB : 3 * SUB + 1, :] * gfs[back_at].astype(F32)
        grads = (
            gq_r[slot],
            (gkv * mixed_r[slot, 2].astype(F32)).astype(BF16),
            (gkv * mixed_r[slot, 1].astype(F32)).astype(BF16),
        )
        last = lax.broadcasted_iota(jnp.int32, (SUB, wide), 0) == SUB - 1
        gs = []
        for i in range(3):
            gmf = grads[i].astype(F32)
            ext = dot(spread_ref[...], xp_r[slot, i])
            rolled = []
            for u in range(lag):
                tile = gmf[u * SUB : (u + 1) * SUB]
                rolled.append(jnp.where(last, 0.0, pltpu.roll(tile, SUB - 1, axis=0)))
                heads[back_at, i, u : u + 1, :] = tile[0:1]
            heads[back_at, i, lag:, :] = jnp.zeros((SUB - lag, wide), F32)
            gme = jnp.concatenate([gmf] + rolled, axis=0)
            total = None
            for j in range(lag + 1):
                term = small[i * SUB + j : i * SUB + j + 1, :] * gme[j * SUB : j * SUB + tokens]
                total = term if total is None else total + term
                at = (lag - j) * SUB
                gs.append(jnp.sum(gmf * ext[at : at + tokens], axis=0, keepdims=True))
            gs += [jnp.zeros((1, wide), F32)] * (SUB - short_len)
            gp_ref[i] = dot_tn(perm_ref[...], total.astype(BF16)).astype(BF16)
        gs.append(jnp.zeros((part_rows - 3 * SUB, wide), F32))
        put_parts(back_at, PARTS - 1, jnp.concatenate(gs, axis=0).astype(BF16))

    share = peers // 4
    for n in range(4):
        @pl.when(grad_at == kept_blocks + 2 + n)
        def _():
            for r in range(n * share, (n + 1) * share):
                part = acc[:, r * features : (r + 1) * features].astype(BF16)
                part = dot_tn(perm_ref[...], part).astype(BF16)
                if aligned:
                    out_ref[:, pl.ds(pl.multiple_of(piece_owner(me, peers, r) * features, features), features)] = part
                else:
                    out_ref[:, r * features : (r + 1) * features] = part

    @pl.when(t == last_step)
    def _():
        @pl.loop(0, units)
        def _(u):
            for k in range(hops):
                both(u, lambda late: when(sends(k, late), lambda: gather(u, k, late).wait_send()))

        if team:
            @pl.loop(0, kept_blocks // team)
            def _(g):
                halves(g).wait_send()
                plane_all(g).wait_send()
                column_all(g).wait_send()
                total_all(g).wait_send()
                totals_all(g).wait_send()
                whole_totals(g).wait_send()

    @pl.when((t == last_step) & has_right)
    def _():
        @pl.loop(0, kept_blocks)
        def _(b):
            kv_copy(b).wait_send()
            head_copy(b).wait_recv()

    @pl.when((t == last_step) & has_left)
    def _():
        @pl.loop(0, kept_blocks)
        def _(b):
            gf_copy(b).wait_send()
            head_copy(b).wait_send()

    @pl.when(t == last_step)
    def _():
        halo_ref[...] = heads_in[...]


def final_kernel(slot_ref, gp_ref, halo_ref, small_ref, red_ref, out_ref, long_ref, short_ref, gain_ref, pad):
    tokens = gp_ref.shape[1]
    taps = long_ref.shape[0]
    short_len = short_ref.shape[1]
    block = slot_ref.shape[2]
    keep = tokens - 2 * SUB
    for n in range(slot_ref.shape[0]):
        to = slice(n * block, (n + 1) * block)
        at = slice(n * block // 2, (n + 1) * block // 2)
        pick = selector(slot_ref[n], block // 2)
        pad[n, 0 : 2 * SUB, :] = jnp.zeros((2 * SUB, block // 2), F32)
        rows = []
        for i in range(3):
            pad[n, 2 * SUB :, :] = halo_ref[n, i]
            fix = None
            for j in range(1, short_len):
                term = small_ref[i * SUB + j : i * SUB + j + 1, at] * pad[n, j : j + 2 * SUB, :]
                fix = term if fix is None else fix + term
            rows += [gp_ref[i, :keep, at], (gp_ref[i, keep:, at].astype(F32) + fix).astype(BF16)]
        rows += [red_ref[:, at]]
        wide_rows = dot(jnp.concatenate(rows, axis=0), pick)
        for i in range(3):
            out_ref[i, :, to] = wide_rows[i * tokens : (i + 1) * tokens].astype(BF16)
        long_ref[:, to] = wide_rows[3 * tokens : 3 * tokens + taps]
        gain_ref[:, to] = wide_rows[3 * tokens + taps : 3 * tokens + taps + 1]
        base = 3 * tokens + red_ref.shape[0] // PARTS * (PARTS - 1)
        for i in range(3):
            short_ref[i, :, to] = wide_rows[base + i * SUB : base + i * SUB + short_len]


def params(flops=0, moved=0):
    return dict(
        compiler_params=pltpu.CompilerParams(
            dimension_semantics=("arbitrary",), vmem_limit_bytes=56 * 2**20
        ),
        cost_estimate=pl.CostEstimate(flops=int(flops), bytes_accessed=int(moved), transcendentals=0),
    )


def local(proj_in, short_taps, long_taps, skip_gain, keep, w_out, grad_out):
    tokens, _, channels = proj_in.shape
    tap_count = long_taps.shape[0]
    short_len = short_taps.shape[0]
    lag = short_len - 1
    size = tokens + tap_count
    block = min(BLOCK, channels)
    wide = block // 2
    blocks = channels // block
    kept = channels // 2

    table = {name: jnp.asarray(value, BF16) for name, value in tables(tokens, tap_count, short_len).items()}

    x = proj_in.transpose(1, 0, 2)
    short = short_taps.transpose(1, 0, 2)
    keep = keep.reshape(blocks, 1, block)
    count = jnp.asarray(np.triu(np.ones((block, block))), BF16)
    gain = skip_gain.reshape(1, channels)
    go = lax.all_gather(grad_out, "chan", axis=1, tiled=True)
    whole = pl.BlockSpec(memory_space=pltpu.VMEM)

    def two(rows, off=0, cols=wide):
        return pl.BlockSpec((rows, cols), lambda c: (0, c + off))

    def three(lead, rows, off=0, at=0, cols=wide):
        return pl.BlockSpec((lead, rows, cols), lambda c: (at, 0, c + off))

    def sds(shape, kind):
        return jax.ShapeDtypeStruct(shape, kind)

    features = w_out.shape[1]
    peers = lax.axis_size("seq")
    per_block = 2
    units = blocks * per_block
    unit_rows = wide // per_block
    group = 4 if blocks % 4 == 0 else 1
    packed, slot = pl.pallas_call(
        pack_kernel,
        grid=(blocks // group,),
        in_specs=[
            pl.BlockSpec((group, 1, block), lambda c: (c, 0, 0)), whole,
            pl.BlockSpec((block * group, features), lambda c: (c, 0)),
        ],
        out_specs=[
            pl.BlockSpec((wide * group, features), lambda c: (c, 0)), pl.BlockSpec((group, 1, block), lambda c: (c, 0, 0)),
        ],
        out_shape=[sds((kept, features), BF16), sds((blocks, 1, block), jnp.int32)],
        name="pack",
        **params(channels * block * features, 3 * channels * features),
    )(keep, count, w_out)
    packed = packed.reshape(units, unit_rows, features)

    me = lax.axis_index("seq")
    owners = jnp.stack([jnp.asarray(piece_owner(me, peers, r), jnp.int32) for r in range(peers)])
    aligned = features % 128 == 0
    if not aligned:
        go = jnp.take(go.reshape(tokens, peers, features), owners, axis=1).reshape(tokens, peers * features)

    edge = shifted(x[:, tokens - EDGE :, :], "seq", 1)
    skew = 3
    ring = min(6, blocks)
    part_rows = (tap_count + SUB + 2 * SUB * (PARTS - 1)) // (2 * SUB * (PARTS - 1)) * 2 * SUB
    team = peers // (2 * PARTS)
    if wide % 256 or team == 0 or blocks % team or peers & (peers - 1) or team * 2 * PARTS != peers:
        team = 0
    teams = blocks // team if team else 1
    slots = peers if team else 1
    hops = 6 if peers == 32 else peers.bit_length() - 1
    total_steps = blocks + skew + 8

    def step(off):
        return lambda t: jnp.minimum(jnp.maximum(t - off, 0), blocks - 1)

    def blk(shape, off):
        at = step(off)
        lead = (0,) * (len(shape) - 1)
        return pl.BlockSpec(shape, lambda t: lead + (at(t),))

    m_off, b_off = skew - 3, skew + 1
    out, gp, halo, red, small = pl.pallas_call(
        functools.partial(mega_kernel, peers, blocks, skew, team),
        grid=(total_steps,),
        in_specs=[
            pl.BlockSpec((1, 1, block), lambda t: (step(m_off)(t), 0, 0)), blk((3, tokens, block), m_off), blk((3, EDGE, block), m_off),
            blk((tap_count, block), m_off), blk((3, short_len, block), m_off), blk((1, block), m_off),
        ] + [whole] * 9 + [pl.BlockSpec(memory_space=pl.ANY)],
        out_specs=[
            whole, blk((3, tokens, wide), b_off), whole, whole, blk((4 * SUB, wide), m_off),
        ],
        out_shape=[
            sds((tokens, peers * features), BF16), sds((3, tokens, kept), BF16), sds((blocks, 3, SUB, wide), F32),
            sds((PARTS * part_rows, kept), BF16), sds((4 * SUB, kept), F32),
        ],
        scratch_shapes=[
            pltpu.VMEM((units, 4, 2, peers // 8, unit_rows, features), BF16),
            pltpu.VMEM((tokens, peers * features), BF16),
            pltpu.VMEM((tokens, peers * features), F32),
            pltpu.VMEM((blocks, tokens, wide), BF16),
            pltpu.VMEM((blocks, tokens, wide), BF16),
            pltpu.VMEM((blocks, tokens, wide), BF16),
            pltpu.VMEM((blocks, tokens, wide), BF16),
            pltpu.VMEM((ring, 3, tokens, wide), BF16),
            pltpu.VMEM((ring, 3, EDGE + tokens, wide), BF16),
            pltpu.VMEM((ring, tokens, wide), BF16),
            pltpu.VMEM((ring, tokens, wide), BF16),
            pltpu.VMEM((ring, size, wide), BF16),
            pltpu.VMEM((ring, size, wide), BF16),
            pltpu.VMEM((ring, size, wide), BF16),
            pltpu.VMEM((ring, tokens, wide), BF16),
            pltpu.VMEM((ring, tap_count, wide), BF16),
            pltpu.VMEM((ring, 4 * SUB, wide), F32),
            pltpu.VMEM((4 * SUB, block), F32),
            pltpu.SemaphoreType.DMA,
            pltpu.SemaphoreType.DMA((units, hops)),
            pltpu.SemaphoreType.DMA((units, hops)),
            pltpu.SemaphoreType.DMA((blocks,)),
            pltpu.SemaphoreType.DMA((blocks,)),
            pltpu.SemaphoreType.DMA((blocks,)),
            pltpu.SemaphoreType.DMA((blocks,)),
            pltpu.VMEM((teams, slots, part_rows, wide // 2), BF16),
            pltpu.VMEM((teams, slots, part_rows, wide // 2), BF16),
            pltpu.VMEM((teams, slots, part_rows, wide // 2), BF16),
            pltpu.SemaphoreType.DMA((teams, 6)),
            pltpu.SemaphoreType.DMA((teams, 6)),
            pltpu.VMEM((blocks, 3, SUB, wide), F32),
            pltpu.SemaphoreType.DMA((blocks,)),
            pltpu.SemaphoreType.DMA((blocks,)),
            pltpu.VMEM((blocks, 3, SUB, wide), F32),
        ],
        compiler_params=pltpu.CompilerParams(
            dimension_semantics=("arbitrary",), vmem_limit_bytes=63 * 2**20, collective_id=0, has_side_effects=True,
        ),
        cost_estimate=pl.CostEstimate(
            flops=4 * tokens * kept * peers * features, bytes_accessed=20 * tokens * channels, transcendentals=0),
        name="mega",
    )(
        slot, x, edge, long_taps, short, gain,
        *[table[k] for k in ("spread", "perm", "own", "own_taps", "before", "after", "inv", "inv_taps")], go, packed,
    )
    if not aligned:
        back = jnp.argsort(owners)
        out = jnp.take(out.reshape(tokens, peers, features), back, axis=1).reshape(tokens, peers * features)
    if not team:
        red = lax.psum(red, "seq")
    summed = lax.psum_scatter(out, "chan", scatter_dimension=1, tiled=True)
    output = summed.astype(F32).astype(BF16)
    pair = 2 if blocks % 2 == 0 else 1
    many, few = pair * block, pair * wide
    grad_proj, grad_long, grad_short, grad_gain = pl.pallas_call(
        final_kernel,
        grid=(blocks // pair,),
        in_specs=[
            pl.BlockSpec((pair, 1, block), lambda c: (c, 0, 0)), three(3, tokens, cols=few),
            pl.BlockSpec((pair, 3, SUB, wide), lambda c: (c, 0, 0, 0)), two(4 * SUB, 0, few), two(PARTS * part_rows, 0, few),
        ],
        out_specs=[three(3, tokens, cols=many), two(tap_count, 0, many), three(3, short_len, cols=many), two(1, 0, many)],
        out_shape=[
            sds((3, tokens, channels), BF16), sds((tap_count, channels), F32), sds((3, short_len, channels), F32),
            sds((1, channels), F32),
        ],
        scratch_shapes=[pltpu.VMEM((pair, 3 * SUB, wide), F32)],
        name="final",
        **params(42 * 16 * channels, 300 * channels),
    )(slot, gp, halo, small, red)
    return (
        output,
        grad_proj.transpose(1, 0, 2),
        grad_long,
        grad_short.transpose(1, 0, 2),
        grad_gain.reshape(channels),
    )


def solution(mesh):
    placed = (
        P("seq", None, "chan"),
        P(None, None, "chan"),
        P(None, "chan"),
        P("chan"),
        P("chan"),
        P("chan", "seq"),
        P("seq", "chan"),
    )
    return jax.shard_map(
        local,
        mesh=mesh,
        in_specs=placed,
        out_specs=(
            P("seq", "chan"),
            P("seq", None, "chan"),
            P(None, "chan"),
            P(None, None, "chan"),
            P("chan"),
        ),
        check_vma=False,
    )
```
